128 devices in a mesh: ctx: 16 (over y_lo, z, core), dp: 8 (over y_hi, x).
Axes of the slice: x: 4, y: 4 (y_hi: 2, y_lo: 2; y = y_hi * 2 + y_lo), z: 4, core: 2. Of those that a mesh axis runs over, the one named last changes fastest.
Arguments:
- hidden: bfloat16 [98304, 1024], P(('dp', 'ctx')), parts along dimension 0, may hold values from -4 to 4
- in_weight: bfloat16 [1024, 4384], replicated, may hold values from -0.1875 to 0.1875
- conv_weight: float32 [4, 2304], replicated, may hold values from -3 to 3
- conv_bias: float32 [2304], replicated, may hold values from -3 to 3
- step_bias: float32 [32], replicated, may hold values from -1 to 1
- decay_rate: float32 [32], replicated, may hold values from 8.138021e-06 to 0.05
- skip_gain: float32 [32], replicated, may hold values from 0.5 to 1.5
- norm_gain: float32 [2048], replicated, may hold values from 0.5 to 1.5
- out_weight: bfloat16 [2048, 1024], replicated, may hold values from -0.125 to 0.125
Outputs:
- mixed: bfloat16 [98304, 1024], P(('dp', 'ctx')), parts along dimension 0
The draws below stay inside these ranges and needn't reach their ends.
There are 8 independent parts, one for each index of `dp`. The reference program is written for one: setup_inputs(seed, part) draws one part's arguments, and reference() takes and returns one part's arrays. A program takes and returns all parts, laid end to end along the dimension named above; an argument that names none is the same for every part. Nothing has to cross between parts.
All inputs are finite; a program needn't handle non-finite values.
Results may differ from the reference program's by a relative error of at most 0.0065.
Values may be sent and summed in bfloat16 or wider, within the bound.
A program may use at most 256 MiB of HBM per device.

```python
import math
import jax
import jax.numpy as jnp
from jax import lax

D = 1024
HEADS = 32
HEAD_DIM = 64
STATE = 128
GROUP = 256
KERNEL = 4
D_INNER = 2048
XBC = 2304
PROJ = 4384
SEQ = 12288


def steps_of(stream_key, dims, cuts, smallest, top_value):
    gain = 1.0
    for dim, blocks in cuts:
        steps = jax.random.uniform(jax.random.fold_in(jax.random.fold_in(stream_key, 6), dim), (blocks,), jnp.float32, smallest / len(cuts), top_value / len(cuts))
        gain = gain * jnp.repeat(jnp.exp(steps), dims[dim] // blocks).reshape((-1,) + (1,) * (len(dims) - 1 - dim))
    return gain


def normal_values(key, shape, scale, most, cuts=(), held_as=jnp.bfloat16):
    values = scale * jax.random.normal(key, shape, jnp.float32)
    if cuts:
        values = values * steps_of(key, shape, cuts, -0.22, 0.18)
    return jnp.clip(values, -most, most).astype(held_as)


def setup_inputs(seed: int = 0, part: int = 0) -> dict:
    key_list = jax.random.split(jax.random.key(seed), 10)
    part_keys = jax.random.split(jax.random.fold_in(key_list[9], part), 10)
    hidden = normal_values(part_keys[0], (SEQ, D), 1.0, 4.0, ((0, 16),))
    in_weight = normal_values(key_list[1], (D, PROJ), D ** -0.5, 0.1875)
    conv_weight = normal_values(key_list[2], (KERNEL, XBC), 0.5, 3.0, (), jnp.float32)
    conv_bias = normal_values(key_list[3], (XBC,), 0.5, 3.0, (), jnp.float32)
    step_bias = jnp.clip(jax.random.uniform(key_list[4], (HEADS,), jnp.float32, -1.0, 1.0), -1.0, 1.0)
    decay_rate = jnp.clip(jnp.exp(jax.random.uniform(key_list[5], (HEADS,), jnp.float32, math.log(8.138021257764194e-06), math.log(0.05))), 8.138021257764194e-06, 0.05)
    skip_gain = jnp.clip(jax.random.uniform(key_list[6], (HEADS,), jnp.float32, 0.5, 1.5), 0.5, 1.5)
    norm_gain = jnp.clip(1.0 + 0.1 * jax.random.normal(key_list[7], (D_INNER,), jnp.float32), 0.5, 1.5)
    out_weight = normal_values(key_list[8], (D_INNER, D), D_INNER ** -0.5, 0.125)
    return dict(hidden=hidden, in_weight=in_weight, conv_weight=conv_weight, conv_bias=conv_bias, step_bias=step_bias, decay_rate=decay_rate, skip_gain=skip_gain, norm_gain=norm_gain, out_weight=out_weight)


def rounded(values):
    return lax.optimization_barrier(values.astype(jnp.bfloat16)).astype(jnp.float32)

def group_terms(xc_block, step_raw, step_bias, decay_rate, skip_gain):
    length = xc_block.shape[0]
    values = xc_block[:, :D_INNER].astype(jnp.float32).reshape(length, HEADS, HEAD_DIM)
    b_matrix = xc_block[:, D_INNER:D_INNER + STATE]
    c_matrix = xc_block[:, D_INNER + STATE:]
    step_size = jax.nn.softplus(step_raw.astype(jnp.float32) + step_bias[None, :])
    log_decay = jnp.cumsum(-step_size * decay_rate[None, :], axis=0)
    scores = jnp.dot(c_matrix, b_matrix.T, preferred_element_type=jnp.float32)
    positions = jnp.arange(length)
    causal = positions[:, None] >= positions[None, :]
    log_gap = jnp.where(causal[None], log_decay.T[:, :, None] - log_decay.T[:, None, :], -jnp.inf)
    mixing = rounded(jnp.exp(log_gap) * scores[None] * step_size.T[:, None, :])
    within = jnp.einsum('hts,shp->thp', mixing, values, precision=lax.Precision.HIGHEST)
    within = within + skip_gain[None, :, None] * values
    to_end = jnp.exp(log_decay[-1][None, :] - log_decay) * step_size
    weighted = rounded(values * to_end[:, :, None])
    summary = jnp.einsum('shp,sn->hpn', weighted, b_matrix.astype(jnp.float32), precision=lax.Precision.HIGHEST)
    return (within, log_decay, summary, c_matrix)

def strand(hidden, in_weight, conv_weight, conv_bias, step_bias, decay_rate, skip_gain, norm_gain, out_weight):
    length = hidden.shape[0]
    projected = jnp.dot(hidden, in_weight, preferred_element_type=jnp.float32).astype(jnp.bfloat16)
    gating = projected[:, :D_INNER]
    conv_in = projected[:, D_INNER:D_INNER + XBC]
    step_raw = projected[:, D_INNER + XBC:]
    padded = jnp.concatenate([jnp.zeros((KERNEL - 1, XBC), jnp.bfloat16), conv_in], 0)
    filtered = jnp.zeros((length, XBC), jnp.float32) + conv_bias[None, :]
    for tap_index in range(KERNEL):
        filtered = filtered + conv_weight[tap_index][None, :] * padded[tap_index:tap_index + length].astype(jnp.float32)
    xc = jax.nn.silu(filtered).astype(jnp.bfloat16)
    group_count = length // GROUP

    def one_group(running, pieces):
        xc_block, step_block = pieces
        within, log_decay, summary, c_matrix = group_terms(xc_block, step_block, step_bias, decay_rate, skip_gain)
        carried = jnp.einsum('tn,hpn->thp', c_matrix.astype(jnp.float32), rounded(running), precision=lax.Precision.HIGHEST)
        carried = carried * jnp.exp(log_decay)[:, :, None]
        new_state = jnp.exp(log_decay[-1])[:, None, None] * running + summary
        return (new_state, within + carried)
    start_state = jnp.zeros((HEADS, HEAD_DIM, STATE), jnp.float32)
    final_state, outputs = lax.scan(one_group, start_state, (xc.reshape(group_count, GROUP, XBC), step_raw.reshape(group_count, GROUP, HEADS)))
    scanned = outputs.reshape(length, D_INNER)
    gated_out = scanned * jax.nn.silu(gating.astype(jnp.float32))
    normed = (gated_out * lax.rsqrt(lax.optimization_barrier(jnp.mean(gated_out * gated_out, axis=-1, keepdims=True)) + 1e-05) * norm_gain[None, :]).astype(jnp.bfloat16)
    return jnp.dot(normed, out_weight, preferred_element_type=jnp.float32).astype(jnp.bfloat16)

def reference(hidden, in_weight, conv_weight, conv_bias, step_bias, decay_rate, skip_gain, norm_gain, out_weight):
    forward = strand(hidden, in_weight, conv_weight, conv_bias, step_bias, decay_rate, skip_gain, norm_gain, out_weight)
    reverse_hidden = jnp.flip(hidden, 0)
    backward = strand(reverse_hidden, in_weight, conv_weight, conv_bias, step_bias, decay_rate, skip_gain, norm_gain, out_weight)
    returned = jnp.flip(backward, 0)
    return (hidden.astype(jnp.float32) + forward.astype(jnp.float32) + returned.astype(jnp.float32)).astype(jnp.bfloat16)
```

```python
import functools

import jax
import jax.numpy as jnp
from jax import lax
from jax.experimental import pallas as pl
from jax.experimental.pallas import tpu as pltpu
from jax.sharding import PartitionSpec as P

CHUNK = 128
TILE = 256
HALO = 8
ROWS = 256
LIMIT = 40.0
MESH = pl.DeviceIdType.MESH
HIGHEST = lax.Precision.HIGHEST
F32 = jnp.float32
BF16 = jnp.bfloat16


def dot(a, b):
    return jnp.dot(a, b, preferred_element_type=F32)


def dot_nt(a, b):
    return lax.dot_general(a, b, (((1,), (1,)), ((), ())), preferred_element_type=F32)


def silu(x):
    half = 0.5 * x
    return half + half * jnp.tanh(half)


def iota(shape, dim):
    return lax.broadcasted_iota(jnp.int32, shape, dim)


def high_low(x, heads):
    high = x.astype(BF16).astype(F32)
    return (high + pltpu.roll(x - high, heads, 1)).astype(BF16)


def spread_matrix(first_head, heads, head_dim, terms):
    row, column = iota((128, TILE), 0), iota((128, TILE), 1)
    head = first_head + lax.div(column, head_dim)
    hit = row == head
    if terms == 2:
        hit = hit | (row == head + heads)
    return jnp.where(hit, 1.0, 0.0)


def triangle(lower):
    row, column = iota((CHUNK, CHUNK), 0), iota((CHUNK, CHUNK), 1)
    return row >= column if lower else row <= column


def front_kernel(
    heads, head_dim, state, inner, x_ref, next_ref, prev_ref, w_ref, wdt_ref, cw_ref, cb_ref, bias_ref, decay_ref, skip_ref,
    gate_ref, xf_ref, xb_ref, yf_ref, yb_ref, sf_ref, sb_ref, end_ref, ef_ref, eb_ref, step_ref, tot_ref, span_ref,
    hx, xs, par, wf, wb, of, ob, gcf, gcb, btf, btb, small,
):
    length = x_ref.shape[0]
    chunks = length // CHUNK
    tiles = inner // TILE
    j = pl.program_id(0)

    def project():
        out = dot(hx[...], w_ref[...])
        xs[HALO : HALO + length] = out[:length]
        xs[HALO + length :] = out[length : length + HALO]
        xs[:HALO] = out[length + HALO :]

    def convolved(c):
        at = HALO + c * CHUNK
        taps = [cw_ref[k : k + 1, :] for k in range(4)]
        base = xs[at : at + CHUNK] * taps[3] + cb_ref[...]
        forward, backward = base, base
        for k in range(1, 4):
            forward = forward + xs[at - k : at - k + CHUNK] * taps[3 - k]
            backward = backward + xs[at + k : at + k + CHUNK] * taps[3 - k]
        return silu(forward), silu(backward)

    @pl.when(j == 0)
    def _():
        hx[:length] = x_ref[...]
        hx[length:] = jnp.concatenate(
            [next_ref[...].astype(F32), prev_ref[...].astype(F32)], 0
        ).astype(BF16)
        par[...] = jnp.zeros_like(par)
        par[0:1, :heads] = bias_ref[...]
        par[1:2, :heads] = decay_ref[...]
        small[...] = jnp.zeros_like(small)
        small[7:8, :heads] = skip_ref[...]
        project()
        raw = dot(hx[:length], wdt_ref[...]).astype(BF16).astype(F32)
        lane = iota((length, 128), 1)
        raw = jnp.where(lane < heads, raw + par[0:1, :], 0.0)
        step = jnp.maximum(raw, 0.0) + jnp.log1p(jnp.exp(-jnp.abs(raw)))
        step = jnp.where(lane < heads, step, 0.0)
        step_ref[...] = step
        rate = -step * par[1:2, :]
        lower = jnp.where(triangle(True), 1.0, 0.0)
        upper = jnp.where(triangle(False), 1.0, 0.0)
        live = iota((CHUNK, 128), 1) < heads
        before = jnp.zeros((1, 128), F32)
        backs, totals = [], []
        for c in range(chunks):
            rows = slice(c * CHUNK, (c + 1) * CHUNK)
            head = jnp.dot(lower, rate[rows], precision=HIGHEST, preferred_element_type=F32)
            tail = jnp.dot(upper, rate[rows], precision=HIGHEST, preferred_element_type=F32)
            total = head[CHUNK - 1 :]
            dt = step[rows]

            def put(ref, value):
                ref[rows, :] = high_low(jnp.where(live, value, 0.0), heads)

            put(wf, dt * jnp.exp(jnp.minimum(total - head, 0.0)))
            put(wb, dt * jnp.exp(jnp.minimum(total - tail, 0.0)))
            put(of, jnp.exp(jnp.minimum(head - total, 80.0)))
            put(ob, jnp.exp(jnp.minimum(tail - total, 80.0)))
            put(ef_ref, jnp.exp(head + before))
            before = before + total
            backs.append(tail)
            totals.append(total)
            tot_ref[c : c + 1, :] = total
            small[c : c + 1, :] = jnp.exp(total)
            span_ref[c] = -jnp.min(total)
        tot_ref[chunks:, :] = jnp.zeros((8 - chunks, 128), F32)
        small[6:7, :] = before
        after = jnp.zeros((1, 128), F32)
        for c in reversed(range(chunks)):
            rows = slice(c * CHUNK, (c + 1) * CHUNK)
            eb_ref[rows, :] = high_low(jnp.where(live, jnp.exp(backs[c] + after), 0.0), heads)
            after = after + totals[c]
        for c in range(chunks):
            rows = slice(c * CHUNK, (c + 1) * CHUNK)
            forward, backward = convolved(c)
            for value, out, gc, bt, keep in (
                (forward, xf_ref, gcf, btf, triangle(True)),
                (backward, xb_ref, gcb, btb, triangle(False)),
            ):
                rounded = value.astype(BF16)
                out[rows, :] = rounded
                b_part, c_part = rounded[:, :state], rounded[:, state:]
                gc[rows, :CHUNK] = jnp.where(keep, dot_nt(c_part, b_part), 0.0).astype(BF16)
                gc[rows, CHUNK:] = c_part
                bt[rows, :] = value[:, :state].T.astype(BF16)

    @pl.when((j > 0) & (j <= tiles))
    def _():
        project()
        first = (j - 1) * (TILE // head_dim)
        spread = spread_matrix(first, heads, head_dim, 2).astype(BF16)
        rows8 = jnp.dot(
            small[...], spread_matrix(first, heads, head_dim, 1), precision=HIGHEST, preferred_element_type=F32
        )
        skip = rows8[7:8]
        weighted_b, y_base = [], []
        running = jnp.zeros((state, TILE), F32)
        for c in range(chunks):
            rows = slice(c * CHUNK, (c + 1) * CHUNK)
            forward, backward = convolved(c)
            xf_ref[rows, :] = forward.astype(BF16)
            xb_ref[rows, :] = backward.astype(BF16)
            scaled = (forward * dot(wf[rows, :], spread)).astype(BF16)
            decayed = running * rows8[c : c + 1]
            sf_ref[c] = running.astype(BF16)
            mixed = dot(gcf[rows, :], jnp.concatenate([scaled, decayed.astype(BF16)], 0))
            yf_ref[rows, :] = (mixed * dot(of[rows, :], spread) + skip * forward).astype(BF16)
            running = decayed + dot(btf[rows, :], scaled)
        ends = [running]
        running = jnp.zeros((state, TILE), F32)
        for c in reversed(range(chunks)):
            rows = slice(c * CHUNK, (c + 1) * CHUNK)
            backward = xb_ref[rows, :].astype(F32)
            scaled = (backward * dot(wb[rows, :], spread)).astype(BF16)
            decayed = running * rows8[c : c + 1]
            sb_ref[c] = running.astype(BF16)
            mixed = dot(gcb[rows, :], jnp.concatenate([scaled, decayed.astype(BF16)], 0))
            yb_ref[rows, :] = (mixed * dot(ob[rows, :], spread) + skip * backward).astype(BF16)
            running = decayed + dot(btb[rows, :], scaled)
        ends.append(running)
        total = rows8[6:7]
        high = total.astype(BF16).astype(F32)
        middle = (total - high).astype(BF16).astype(F32)
        low = total - high - middle
        extra = jnp.concatenate([high, middle, low, jnp.zeros((13, TILE), F32)], 0).astype(BF16)
        for strand in range(2):
            for half in range(TILE // 128):
                lanes = slice(half * 128, (half + 1) * 128)
                end_ref[half, strand, :state, :] = ends[strand][:, lanes].astype(BF16)
                end_ref[half, strand, state:, :] = extra[:, lanes]

    @pl.when(j > tiles)
    def _():
        gate_ref[...] = dot(x_ref[...], w_ref[...]).astype(BF16)


def carry_kernel(end_ref, in_ref, arrived, answers, out_sem, in_sem, out_sem2, in_sem2, own_sem):
    count = end_ref.shape[0]
    state = in_ref.shape[2]
    me = lax.axis_index("ctx")
    barrier = pltpu.get_barrier_semaphore()
    peers = [lax.rem(me + d, count) for d in range(1, count)]
    for peer in peers:
        pl.semaphore_signal(barrier, inc=1, device_id={"ctx": peer}, device_id_type=MESH)
    pl.semaphore_wait(barrier, count - 1)

    def send(src, dst, sems, sem_to, peer):
        return pltpu.make_async_remote_copy(
            src_ref=src, dst_ref=dst, send_sem=sems, recv_sem=sem_to, device_id={"ctx": peer}, device_id_type=MESH
        )

    first = [send(end_ref.at[p], arrived.at[me], out_sem.at[p], in_sem.at[me], p) for p in peers]
    for copy in first:
        copy.start()
    own = pltpu.make_async_copy(end_ref.at[me], arrived.at[me], own_sem.at[0])
    own.start()
    own.wait()
    for p in peers:
        send(end_ref.at[p], arrived.at[p], out_sem.at[p], in_sem.at[p], p).wait_recv()

    def factor(k):
        rows = arrived[k, 0, state : state + 16, :].astype(F32)
        return jnp.exp(rows[0:1] + rows[1:2] + rows[2:3])

    running = jnp.zeros((state, 128), F32)
    for k in range(count):
        answers[k, 0] = running.astype(BF16)
        if k < count - 1:
            running = factor(k) * running + arrived[k, 0, :state, :].astype(F32)
    running = jnp.zeros((state, 128), F32)
    for k in reversed(range(count)):
        answers[k, 1] = running.astype(BF16)
        if k > 0:
            running = factor(k) * running + arrived[k, 1, :state, :].astype(F32)
    second = [send(answers.at[p], in_ref.at[me], out_sem2.at[p], in_sem2.at[me], p) for p in peers]
    for copy in second:
        copy.start()
    own = pltpu.make_async_copy(answers.at[me], in_ref.at[me], own_sem.at[1])
    own.start()
    own.wait()
    for p in peers:
        send(answers.at[p], in_ref.at[p], out_sem2.at[p], in_sem2.at[p], p).wait_recv()
    for copy in first:
        copy.wait_send()
    for copy in second:
        copy.wait_send()


def back_kernel(
    heads, head_dim, state, inner, span_ref, yf_ref, yb_ref, gate_ref, cf_ref, cb_ref, ef_ref, eb_ref, in_ref, x_ref,
    w_ref, gain_ref, decay_ref, skip_ref, tot_ref, xf_any, xb_any, sf_any, sb_any, step_any,
    out_ref, gf, gb, accf, accb, normed, par, xbuf, sbuf, dtbuf, sem,
):
    rows = out_ref.shape[0]
    i = pl.program_id(0)
    per_block = rows // CHUNK
    worst = span_ref[i * per_block]
    for k in range(1, per_block):
        worst = jnp.maximum(worst, span_ref[i * per_block + k])

    @pl.when(worst <= LIMIT)
    def _():
        total_f = jnp.zeros((rows, 128), F32)
        total_b = jnp.zeros((rows, 128), F32)
        for j in range(inner // TILE):
            lanes = slice(j * TILE, (j + 1) * TILE)
            spread = spread_matrix(j * (TILE // head_dim), heads, head_dim, 2).astype(BF16)
            gate = silu(gate_ref[:, lanes].astype(F32))

            def strand(y_ref, c_ref, e_ref, s, g):
                entering = jnp.concatenate([in_ref[2 * j, s], in_ref[2 * j + 1, s]], 1)
                y = y_ref[:, lanes].astype(F32) + dot(e_ref[...], spread) * dot(c_ref[...], entering)
                y = y * gate
                g[:, lanes] = y
                square = y * y
                return square[:, :128] + square[:, 128:]

            total_f = total_f + strand(yf_ref, cf_ref, ef_ref, 0, gf)
            total_b = total_b + strand(yb_ref, cb_ref, eb_ref, 1, gb)
        accf[...] = total_f
        accb[...] = total_b

    @pl.when(jnp.logical_not(worst <= LIMIT))
    def _():
        par[...] = jnp.zeros_like(par)
        par[0:1, :heads] = decay_ref[...]
        par[1:2, :heads] = skip_ref[...]
        accf[...] = jnp.zeros_like(accf)
        accb[...] = jnp.zeros_like(accb)
        for s, (x_any, s_any, g, acc) in enumerate(((xf_any, sf_any, gf, accf), (xb_any, sb_any, gb, accb))):
            keep = triangle(s == 0)
            ones = jnp.where(keep, 1.0, 0.0)

            def one_chunk(k, _):
                c = i * per_block + k
                copies = [
                    pltpu.make_async_copy(x_any.at[pl.ds(c * CHUNK, CHUNK)], xbuf, sem.at[0]),
                    pltpu.make_async_copy(s_any.at[c], sbuf, sem.at[1]),
                    pltpu.make_async_copy(step_any.at[pl.ds(c * CHUNK, CHUNK)], dtbuf, sem.at[2]),
                ]
                for copy in copies:
                    copy.start()
                for copy in copies:
                    copy.wait()
                at = pl.ds(pl.multiple_of(k * CHUNK, CHUNK), CHUNK)
                dt = dtbuf[...]
                log_decay = jnp.dot(ones, -dt * par[0:1, :], precision=HIGHEST, preferred_element_type=F32)
                number = iota((8, 128), 0)
                counted = (number < c) if s == 0 else (number > c)
                offset = jnp.sum(jnp.where(counted, tot_ref[...], 0.0), 0, keepdims=True)
                log_t, dt_t = log_decay.T, dt.T
                b_part, c_part = xbuf[:, inner : inner + state], xbuf[:, inner + state :]
                scores = dot_nt(c_part, b_part)
                lane, sub = iota((CHUNK, 128), 1), iota((128, CHUNK), 0)
                lane1 = iota((1, 128), 1)
                left = lane < head_dim

                def pair(q, _):
                    cols = pl.ds(pl.multiple_of(q * 128, 128), 128)
                    v = xbuf[:, cols]
                    outs, ups, skips, offsets = [], [], [], []
                    for half in range(2):
                        h = 2 * q + half
                        column = jnp.sum(jnp.where(lane == h, log_decay, 0.0), 1, keepdims=True)
                        line = jnp.sum(jnp.where(sub == h, log_t, 0.0), 0, keepdims=True)
                        dt_line = jnp.sum(jnp.where(sub == h, dt_t, 0.0), 0, keepdims=True)
                        decay = jnp.where(keep, jnp.exp(jnp.minimum(column - line, 0.0)), 0.0)
                        outs.append(dot((decay * scores * dt_line).astype(BF16), v))
                        ups.append(jnp.exp(column))
                        skips.append(jnp.sum(jnp.where(lane1 == h, par[1:2, :], 0.0), 1, keepdims=True))
                        offsets.append(jnp.sum(jnp.where(lane1 == h, offset, 0.0), 1, keepdims=True))
                    shift = jnp.where(lane1 < head_dim, offsets[0], offsets[1])
                    entering = sbuf[:, cols].astype(F32) + jnp.exp(shift) * in_ref[q, s].astype(F32)
                    carried = dot(c_part, entering.astype(BF16))
                    y = jnp.where(left, outs[0], outs[1]) + jnp.where(left, ups[0], ups[1]) * carried
                    y = y + jnp.where(lane1 < head_dim, skips[0], skips[1]) * v.astype(F32)
                    y = y * silu(gate_ref[at, cols].astype(F32))
                    g[at, cols] = y
                    acc[at, :] += y * y
                    return 0

                lax.fori_loop(0, heads // 2, pair, 0)
                return 0

            lax.fori_loop(0, per_block, one_chunk, 0)

    scale_f = lax.rsqrt(jnp.sum(accf[...], 1, keepdims=True) * (1.0 / inner) + 1e-05)
    scale_b = lax.rsqrt(jnp.sum(accb[...], 1, keepdims=True) * (1.0 / inner) + 1e-05)
    for j in range(inner // TILE):
        lanes = slice(j * TILE, (j + 1) * TILE)
        value = (gf[:, lanes] * scale_f + gb[:, lanes] * scale_b) * gain_ref[:, lanes]
        normed[:, lanes] = value.astype(BF16)
    out_ref[...] = (x_ref[...].astype(F32) + dot(normed[...], w_ref[...])).astype(BF16)


def local(hidden, in_weight, conv_weight, conv_bias, step_bias, decay_rate, skip_gain, norm_gain, out_weight):
    length, width = hidden.shape
    heads = step_bias.shape[0]
    inner = out_weight.shape[0]
    head_dim = inner // heads
    conv_width = conv_weight.shape[1]
    state = (conv_width - inner) // 2
    chunks = length // CHUNK
    tiles = inner // TILE
    count = lax.axis_size("ctx")
    ring = range(count)
    prev = lax.ppermute(hidden[length - HALO :], "ctx", [(i, i + 1) for i in ring if i + 1 < count])
    follow = lax.ppermute(hidden[:HALO], "ctx", [(i + 1, i) for i in ring if i + 1 < count])
    sizes = (heads, head_dim, state, inner)

    def whole(shape, **kw):
        return pl.BlockSpec(shape, lambda j: (0,) * len(shape), **kw)

    def value_tile(j):
        return jnp.clip(j - 1, 0, tiles - 1)

    def conv_tile(j):
        return jnp.where(j == 0, tiles, value_tile(j))

    def weight_tile(j):
        return jnp.where(j == 0, 2 * tiles, jnp.where(j <= tiles, tiles - 1 + j, j - tiles - 1))

    def shape(dims, dtype):
        return jax.ShapeDtypeStruct(dims, dtype)

    row2 = lambda a: a.reshape(1, -1)
    once = dict(pipeline_mode=pl.Buffered(1))
    outs = pl.pallas_call(
        functools.partial(front_kernel, *sizes),
        name="front",
        grid=(1 + 2 * tiles,),
        in_specs=[
            whole((length, width), **once),
            whole((HALO, width)),
            whole((HALO, width)),
            pl.BlockSpec((width, TILE), lambda j: (0, weight_tile(j))),
            pl.BlockSpec((width, 128), lambda j: (0, (inner + conv_width) // 128), **once),
            pl.BlockSpec((4, TILE), lambda j: (0, conv_tile(j))),
            pl.BlockSpec((1, TILE), lambda j: (0, conv_tile(j))),
            whole((1, heads)),
            whole((1, heads)),
            whole((1, heads)),
        ],
        out_specs=[
            pl.BlockSpec((length, TILE), lambda j: (0, jnp.maximum(j - tiles - 1, 0))),
            pl.BlockSpec((length, TILE), lambda j: (0, conv_tile(j))),
            pl.BlockSpec((length, TILE), lambda j: (0, conv_tile(j))),
            pl.BlockSpec((length, TILE), lambda j: (0, value_tile(j))),
            pl.BlockSpec((length, TILE), lambda j: (0, value_tile(j))),
            pl.BlockSpec((chunks, state, TILE), lambda j: (0, 0, value_tile(j))),
            pl.BlockSpec((chunks, state, TILE), lambda j: (0, 0, value_tile(j))),
            pl.BlockSpec((TILE // 128, 2, state + 16, 128), lambda j: (value_tile(j), 0, 0, 0)),
            whole((length, 128)),
            whole((length, 128)),
            whole((length, 128)),
            whole((8, 128)),
            pl.BlockSpec(memory_space=pltpu.SMEM),
        ],
        out_shape=[
            shape((length, inner), BF16),
            shape((length, conv_width), BF16),
            shape((length, conv_width), BF16),
            shape((length, inner), BF16),
            shape((length, inner), BF16),
            shape((chunks, state, inner), BF16),
            shape((chunks, state, inner), BF16),
            shape((inner // 128, 2, state + 16, 128), BF16),
            shape((length, 128), BF16),
            shape((length, 128), BF16),
            shape((length, 128), F32),
            shape((8, 128), F32),
            shape((8,), F32),
        ],
        scratch_shapes=[
            pltpu.VMEM((length + 2 * HALO, width), BF16),
            pltpu.VMEM((length + 2 * HALO, TILE), F32),
            pltpu.VMEM((8, 128), F32),
        ]
        + [pltpu.VMEM((length, 128), BF16)] * 4
        + [pltpu.VMEM((length, CHUNK + state), BF16)] * 2
        + [pltpu.VMEM((chunks * state, CHUNK), BF16)] * 2
        + [pltpu.VMEM((8, 128), F32)],
        compiler_params=pltpu.CompilerParams(vmem_limit_bytes=48 << 20),
    )(
        hidden, follow, prev, in_weight, in_weight, conv_weight, row2(conv_bias), row2(step_bias), row2(decay_rate),
        row2(skip_gain),
    )
    gate, xf, xb, yf, yb, sf, sb, end, ef, eb, step, tot, span = outs
    entering = pl.pallas_call(
        carry_kernel,
        name="carry",
        in_specs=[pl.BlockSpec(memory_space=pltpu.VMEM)],
        out_specs=pl.BlockSpec(memory_space=pltpu.VMEM),
        out_shape=shape((count, 2, state, 128), BF16),
        scratch_shapes=[
            pltpu.VMEM((count, 2, state + 16, 128), BF16),
            pltpu.VMEM((count, 2, state, 128), BF16),
            pltpu.SemaphoreType.DMA((count,)),
            pltpu.SemaphoreType.DMA((count,)),
            pltpu.SemaphoreType.DMA((count,)),
            pltpu.SemaphoreType.DMA((count,)),
            pltpu.SemaphoreType.DMA((2,)),
        ],
        compiler_params=pltpu.CompilerParams(collective_id=0, has_side_effects=True),
    )(end)
    anywhere = pl.BlockSpec(memory_space=pl.ANY)
    block = pl.BlockSpec((ROWS, inner), lambda j: (j, 0))
    c_block = pl.BlockSpec((ROWS, state), lambda j: (j, inner // state + 1))
    e_block = pl.BlockSpec((ROWS, 128), lambda j: (j, 0))
    return pl.pallas_call(
        functools.partial(back_kernel, *sizes),
        name="back",
        grid=(length // ROWS,),
        in_specs=[
            pl.BlockSpec(memory_space=pltpu.SMEM),
            block, block, block, c_block, c_block, e_block, e_block,
            whole((count, 2, state, 128), **once),
            pl.BlockSpec((ROWS, width), lambda j: (j, 0)),
            whole((inner, width), **once),
            whole((1, inner)),
            whole((1, heads)),
            whole((1, heads)),
            whole((8, 128)),
        ]
        + [anywhere] * 5,
        out_specs=pl.BlockSpec((ROWS, width), lambda j: (j, 0)),
        out_shape=shape((length, width), BF16),
        scratch_shapes=[
            pltpu.VMEM((ROWS, inner), F32),
            pltpu.VMEM((ROWS, inner), F32),
            pltpu.VMEM((ROWS, 128), F32),
            pltpu.VMEM((ROWS, 128), F32),
            pltpu.VMEM((ROWS, inner), BF16),
            pltpu.VMEM((8, 128), F32),
            pltpu.VMEM((CHUNK, conv_width), BF16),
            pltpu.VMEM((state, inner), BF16),
            pltpu.VMEM((CHUNK, 128), F32),
            pltpu.SemaphoreType.DMA((3,)),
        ],
        compiler_params=pltpu.CompilerParams(vmem_limit_bytes=56 << 20),
    )(
        span, yf, yb, gate, xf, xb, ef, eb, entering, hidden, out_weight, row2(norm_gain), row2(decay_rate),
        row2(skip_gain), tot, xf, xb, sf, sb, step,
    )


def solution(mesh):
    return jax.shard_map(
        local,
        mesh=mesh,
        in_specs=(P(("dp", "ctx"), None), P(), P(), P(), P(), P(), P(), P(), P()),
        out_specs=P(("dp", "ctx"), None),
        check_vma=False,
    )
```

```python
import functools

import jax
import jax.numpy as jnp
from jax import lax
from jax.experimental import pallas as pl
from jax.experimental.pallas import tpu as pltpu
from jax.sharding import PartitionSpec as P

CHUNK = 128
TILE = 256
HALO = 8
ROWS = 256
LIMIT = 40.0
VMEM = 66_000_000
MESH = pl.DeviceIdType.MESH
HIGHEST = lax.Precision.HIGHEST
F32 = jnp.float32
BF16 = jnp.bfloat16


def dot(a, b):
    return jnp.dot(a, b, preferred_element_type=F32)


def dot_nt(a, b):
    return lax.dot_general(a, b, (((1,), (1,)), ((), ())), preferred_element_type=F32)


def silu(x):
    half = 0.5 * x
    return half + half * jnp.tanh(half)


def iota(shape, dim):
    return lax.broadcasted_iota(jnp.int32, shape, dim)


def iota_mod(shape, dim, mod):
    return lax.rem(iota(shape, dim), mod)


def time_of(index):
    return lax.rem(index, 8) * (CHUNK // 8) + lax.div(index, 8)


def triangle(lower):
    row, column = time_of(iota((CHUNK, CHUNK), 0)), time_of(iota((CHUNK, CHUNK), 1))
    return row >= column if lower else row <= column


def shuffle(inverse):
    row, column = iota((CHUNK, CHUNK), 0), iota((CHUNK, CHUNK), 1)
    hit = row == time_of(column) if inverse else time_of(row) == column
    return jnp.where(hit, 1.0, 0.0).astype(BF16)


def high_low(x):
    high = x.astype(BF16)
    return jnp.concatenate([high, (x - high.astype(F32)).astype(BF16)], 1)


def three_terms(x):
    high = x.astype(BF16).astype(F32)
    middle = (x - high).astype(BF16).astype(F32)
    return [high, middle, x - high - middle]


def spread_matrix(first, head_dim, depth):
    row, column = iota_mod((depth, TILE), 0, 128), iota((depth, TILE), 1)
    return jnp.where(row == first + lax.div(column, head_dim), 1.0, 0.0).astype(BF16)


def front_kernel(
    heads, head_dim, state, inner, x_ref, next_ref, prev_ref, w_ref, wdt_ref, cw_ref, cb_ref, bias_ref, decay_ref, skip_ref,
    gate_ref, xf_ref, xb_ref, yf_ref, yb_ref, sf_ref, sb_ref, end_ref, ef_ref, eb_ref, step_ref, off_ref, span_ref,
    hx, xs, par, wf, wb, of, ob, gcf, gcb, btf, btb, small, rhsf, rhsb,
):
    length = x_ref.shape[0]
    chunks = length // CHUNK
    tiles = inner // TILE
    packs = 128 // heads
    groups = off_ref.shape[0] // 4
    edge = 24
    span = CHUNK + 2 * edge
    j = pl.program_id(0)

    def project():
        out = dot_nt(hx[...], w_ref[...])
        for c in range(chunks):
            xs[c * span + edge : c * span + edge + CHUNK] = out[c * CHUNK : (c + 1) * CHUNK]
        sub = iota((8, TILE), 0)

        def rolled(c, r, by):
            at = c * span + edge + r * 8
            return pltpu.roll(xs[at : at + 8], by, 0)

        for p in range(3):
            r = CHUNK // 8 - 3 + p
            before = jnp.broadcast_to(out[length + 2 * HALO - 3 + p : length + 2 * HALO - 2 + p], (8, TILE))
            for c in range(chunks):
                mine = rolled(c, r, 1)
                xs[c * span + p * 8 : c * span + p * 8 + 8] = jnp.where(sub == 0, before, mine)
                before = mine
            after = jnp.broadcast_to(out[length + p : length + p + 1], (8, TILE))
            for c in reversed(range(chunks)):
                mine = rolled(c, p, 7)
                at = c * span + edge + CHUNK + p * 8
                xs[at : at + 8] = jnp.where(sub == 7, after, mine)
                after = mine

    def convolved(c):
        at = c * span + edge
        taps = [cw_ref[k : k + 1, :] for k in range(4)]
        base = xs[at : at + CHUNK] * taps[3] + cb_ref[...]
        forward, backward = base, base
        for k in range(1, 4):
            forward = forward + xs[at - 8 * k : at - 8 * k + CHUNK] * taps[3 - k]
            backward = backward + xs[at + 8 * k : at + 8 * k + CHUNK] * taps[3 - k]
        return silu(forward), silu(backward)

    @pl.when(j == 0)
    def _():
        order = shuffle(False)
        for c in range(chunks):
            rows = slice(c * CHUNK, (c + 1) * CHUNK)
            hx[rows] = dot(order, x_ref[rows]).astype(BF16)
        hx[length:] = jnp.concatenate(
            [next_ref[...].astype(F32), prev_ref[...].astype(F32)], 0
        ).astype(BF16)
        par[...] = jnp.zeros_like(par)
        for q in range(packs):
            par[0:1, q * heads : (q + 1) * heads] = bias_ref[...]
            par[1:2, q * heads : (q + 1) * heads] = decay_ref[...]
        par[2:3, :heads] = skip_ref[...]
        project()
        lower = jnp.where(triangle(True), 1.0, 0.0)
        upper = jnp.where(triangle(False), 1.0, 0.0)
        lane1 = iota((1, 128), 1)
        wdt = wdt_ref[...]
        zero = jnp.zeros((128, wdt.shape[1]), BF16)
        totals, kept = [], []
        for g in range(groups):
            members = range(g * packs, min((g + 1) * packs, chunks))
            raw = jnp.zeros((CHUNK, 128), F32)
            for q, c in enumerate(members):
                parts = [zero[: q * heads], wdt, zero[: 128 - (q + 1) * heads]]
                wide = jnp.concatenate([p for p in parts if p.shape[0]], 0)
                raw = raw + dot_nt(hx[c * CHUNK : (c + 1) * CHUNK], wide)
            raw = raw.astype(BF16).astype(F32) + par[0:1, :]
            step = jnp.maximum(raw, 0.0) + jnp.log1p(jnp.exp(-jnp.abs(raw)))
            step = jnp.where(iota((CHUNK, 128), 1) < len(members) * heads, step, 0.0)
            step_ref[g] = step
            rate = -step * par[1:2, :]
            head = jnp.dot(lower, rate, precision=HIGHEST, preferred_element_type=F32)
            tail = jnp.dot(upper, rate, precision=HIGHEST, preferred_element_type=F32)
            total = head[CHUNK - 1 :]
            wf[g] = high_low(step * jnp.exp(jnp.minimum(total - head, 0.0)))
            wb[g] = high_low(step * jnp.exp(jnp.minimum(total - tail, 0.0)))
            of[g] = high_low(jnp.exp(jnp.minimum(head - total, 80.0)))
            ob[g] = high_low(jnp.exp(jnp.minimum(tail - total, 80.0)))
            totals.append(total)
            kept.append((head, tail))
            span_ref[g] = -jnp.min(total)

        def wide8(x):
            return jnp.broadcast_to(x, (8, 128))

        def both(x):
            w = wide8(x)
            for q in range(1, packs):
                w = w + pltpu.roll(wide8(x), q * heads, 1)
            return w[0:1]

        lane8 = iota((8, 128), 1)
        sums = [both(t) for t in totals]
        slab = sums[0]
        for t in sums[1:]:
            slab = slab + t
        for g in range(groups):
            t8 = wide8(totals[g])
            early, late = jnp.zeros((8, 128), F32), jnp.zeros((8, 128), F32)
            for q in range(1, packs):
                early = early + jnp.where(lane8 >= q * heads, pltpu.roll(t8, q * heads, 1), 0.0)
                late = late + jnp.where(lane8 < 128 - q * heads, pltpu.roll(t8, 128 - q * heads, 1), 0.0)
            early, late = early[0:1], late[0:1]
            for k in range(groups):
                if k < g:
                    early = early + sums[k]
                if k > g:
                    late = late + sums[k]
            off_ref[g : g + 1, :] = early
            off_ref[groups + g : groups + g + 1, :] = late
            off_ref[2 * groups + 2 * g : 2 * groups + 2 * g + 2, :] = jnp.zeros((2, 128), F32)
            ef_ref[g] = high_low(jnp.exp(kept[g][0] + early))
            eb_ref[g] = high_low(jnp.exp(kept[g][1] + late))
        lines = []
        for g in range(groups):
            lines += three_terms(jnp.exp(totals[g]))
        lines += three_terms(slab) + three_terms(par[2:3, :])
        lines.append(jnp.zeros((16 - len(lines), 128), F32))
        small[...] = jnp.concatenate(lines, 0).astype(BF16)
        for c in range(chunks):
            rows = slice(c * CHUNK, (c + 1) * CHUNK)
            forward, backward = convolved(c)
            for value, out, gc, bt, keep in (
                (forward, xf_ref, gcf, btf, triangle(True)),
                (backward, xb_ref, gcb, btb, triangle(False)),
            ):
                rounded = value.astype(BF16)
                out[rows, :] = rounded
                b_part, c_part = rounded[:, :state], rounded[:, state:]
                gc[rows, :CHUNK] = jnp.where(keep, dot_nt(c_part, b_part), 0.0).astype(BF16)
                gc[rows, CHUNK:] = c_part
                bt[rows, :] = value[:, :state].T.astype(BF16)

    @pl.when((j > 0) & (j <= tiles))
    def _():
        project()
        first = (j - 1) * (TILE // head_dim)
        spreads = [spread_matrix(first + q * heads, head_dim, 256) for q in range(packs)]
        lines = [dot(small[...], spread[:128]) for spread in spreads]

        def line(q, k):
            rows = lines[q][3 * k : 3 * k + 3]
            return rows[0:1] + rows[1:2] + rows[2:3]

        fade = [line(c % packs, c // packs) for c in range(chunks)]
        slab, skip = line(0, groups), line(0, groups + 1)
        for c in range(chunks):
            rows = slice(c * CHUNK, (c + 1) * CHUNK)
            g, spread = c // packs, spreads[c % packs]
            forward, backward = convolved(c)
            xf_ref[rows, :] = forward.astype(BF16)
            xb_ref[rows, :] = backward.astype(BF16)
            rhsf[c, :CHUNK] = (forward * dot(wf[g], spread)).astype(BF16)
            rhsb[c, :CHUNK] = (backward * dot(wb[g], spread)).astype(BF16)
        ends = []
        for order, s_ref, bt, rhs in (
            (range(chunks), sf_ref, btf, rhsf),
            (reversed(range(chunks)), sb_ref, btb, rhsb),
        ):
            running = jnp.zeros((state, TILE), F32)
            for c in order:
                rows = slice(c * CHUNK, (c + 1) * CHUNK)
                decayed = running * fade[c]
                s_ref[c] = running.astype(BF16)
                rhs[c, CHUNK:] = decayed.astype(BF16)
                running = decayed + dot(bt[rows, :], rhs[c, :CHUNK])
            ends.append(running)
        extra = jnp.concatenate(three_terms(slab) + [jnp.zeros((13, TILE), F32)], 0).astype(BF16)
        for strand in range(2):
            for half in range(TILE // 128):
                lanes = slice(half * 128, (half + 1) * 128)
                end_ref[half, strand, :state, :] = ends[strand][:, lanes].astype(BF16)
                end_ref[half, strand, state:, :] = extra[:, lanes]
        for c in range(chunks):
            rows = slice(c * CHUNK, (c + 1) * CHUNK)
            g, spread = c // packs, spreads[c % packs]
            for y_ref, x_out, gc, rhs, o in (
                (yf_ref, xf_ref, gcf, rhsf, of),
                (yb_ref, xb_ref, gcb, rhsb, ob),
            ):
                mixed = dot(gc[rows, :], rhs[c])
                y_ref[rows, :] = (mixed * dot(o[g], spread) + skip * x_out[rows, :].astype(F32)).astype(BF16)

    @pl.when(j > tiles)
    def _():
        gate_ref[...] = dot_nt(hx[:length], w_ref[...]).astype(BF16)


def carry_kernel(
    end_ref, in_ref, paired, chip, arrived, answers, entering, other, out_sem, in_sem, out_sem2, in_sem2, pair_out, pair_in,
    own_sem,
):
    pairs = end_ref.shape[0]
    state = in_ref.shape[2]
    count = pairs // 2
    me = lax.axis_index("ctx")
    core, mine = lax.rem(me, 2), lax.div(me, 2)
    partner = me + 1 - 2 * core
    barrier = pltpu.get_barrier_semaphore()
    chips = [lax.rem(mine + d, count) for d in range(1, count)]
    for peer in [partner] + [2 * k + core for k in chips]:
        pl.semaphore_signal(barrier, inc=1, device_id={"ctx": peer}, device_id_type=MESH)
    pl.semaphore_wait(barrier, count)

    def send(src, dst, sems, sem_to, peer):
        return pltpu.make_async_remote_copy(
            src_ref=src, dst_ref=dst, send_sem=sems, recv_sem=sem_to, device_id={"ctx": peer}, device_id_type=MESH
        )

    swap = send(
        end_ref.at[pl.ds((1 - core) * count, count)], paired, pair_out.at[0], pair_in.at[0], partner
    )
    swap.start()
    swap.wait()

    def total(ref, k):
        rows = ref[k, 0, state : state + 16, :].astype(F32)
        return rows[0:1] + rows[1:2] + rows[2:3]

    low = core == 0

    for k in range(count):
        at = core * count + k
        t_own, t_part = total(end_ref, at), total(paired, k)
        f_own, f_part = jnp.exp(t_own), jnp.exp(t_part)
        one = jnp.ones_like(f_own)
        own0, part0 = end_ref[at, 0, :state, :].astype(F32), paired[k, 0, :state, :].astype(F32)
        own1, part1 = end_ref[at, 1, :state, :].astype(F32), paired[k, 1, :state, :].astype(F32)
        ahead, behind = jnp.where(low, f_part, one), jnp.where(low, one, f_own)
        chip[k, 0, :state, :] = (own0 * ahead + part0 * behind).astype(BF16)
        ahead, behind = jnp.where(low, one, f_part), jnp.where(low, f_own, one)
        chip[k, 1, :state, :] = (own1 * ahead + part1 * behind).astype(BF16)
        extra = jnp.concatenate(three_terms(t_own + t_part) + [jnp.zeros((13, 128), F32)], 0).astype(BF16)
        chip[k, 0, state:, :] = extra
        chip[k, 1, state:, :] = extra
    first = [send(chip.at[k], arrived.at[mine], out_sem.at[k], in_sem.at[mine], 2 * k + core) for k in chips]
    for copy in first:
        copy.start()
    own = pltpu.make_async_copy(chip.at[mine], arrived.at[mine], own_sem.at[0])
    own.start()
    own.wait()
    for k in chips:
        send(chip.at[k], arrived.at[k], out_sem.at[k], in_sem.at[k], 2 * k + core).wait_recv()
    for strand, order in ((0, list(range(count))), (1, list(reversed(range(count))))):
        running = jnp.zeros((state, 128), F32)
        for k in order:
            answers[k, strand] = running.astype(BF16)
            if k != order[-1]:
                running = jnp.exp(total(arrived, k)) * running + arrived[k, strand, :state, :].astype(F32)
    second = [send(answers.at[k], entering.at[mine], out_sem2.at[k], in_sem2.at[mine], 2 * k + core) for k in chips]
    for copy in second:
        copy.start()
    own = pltpu.make_async_copy(answers.at[mine], entering.at[mine], own_sem.at[1])
    own.start()
    own.wait()
    for k in chips:
        send(answers.at[k], entering.at[k], out_sem2.at[k], in_sem2.at[k], 2 * k + core).wait_recv()
    for k in range(count):
        at = core * count + k
        f_own, f_part = jnp.exp(total(end_ref, at)), jnp.exp(total(paired, k))
        chip_f, chip_b = entering[k, 0].astype(F32), entering[k, 1].astype(F32)
        own_late_f = f_part * chip_f + paired[k, 0, :state, :].astype(F32)
        part_late_f = f_own * chip_f + end_ref[at, 0, :state, :].astype(F32)
        own_late_b = f_part * chip_b + paired[k, 1, :state, :].astype(F32)
        part_late_b = f_own * chip_b + end_ref[at, 1, :state, :].astype(F32)
        in_ref[at, 0] = jnp.where(low, chip_f, own_late_f).astype(BF16)
        other[k, 0] = jnp.where(low, part_late_f, chip_f).astype(BF16)
        in_ref[at, 1] = jnp.where(low, own_late_b, chip_b).astype(BF16)
        other[k, 1] = jnp.where(low, chip_b, part_late_b).astype(BF16)
    swap_back = send(other, in_ref.at[pl.ds(core * count, count)], pair_out.at[1], pair_in.at[1], partner)
    swap_back.start()
    swap_back.wait()
    for copy in first:
        copy.wait_send()
    for copy in second:
        copy.wait_send()


def back_kernel(
    heads, head_dim, state, inner, span_ref, yf_ref, yb_ref, gate_ref, cf_ref, cb_ref, ef_ref, eb_ref, in_ref, x_ref,
    w_ref, gain_ref, decay_ref, skip_ref, off_ref, xf_any, xb_any, sf_any, sb_any, step_any,
    out_ref, gf, gb, accf, accb, normed, par, xbuf, sbuf, dtbuf, sem,
):
    rows = out_ref.shape[0]
    i = pl.program_id(0)
    per_block = rows // CHUNK
    packs = 128 // heads
    groups = off_ref.shape[0] // 4
    group = lax.div(i * per_block, packs)
    slot = lax.rem(i * per_block, packs)
    worst = span_ref[group]

    @pl.when(worst <= LIMIT)
    def _():
        total_f = jnp.zeros((rows, 128), F32)
        total_b = jnp.zeros((rows, 128), F32)
        for j in range(inner // TILE):
            lanes = slice(j * TILE, (j + 1) * TILE)
            first = j * (TILE // head_dim)
            spreads = [spread_matrix(first + (slot + k) * heads, head_dim, 256) for k in range(per_block)]
            gate = silu(gate_ref[:, lanes].astype(F32))

            def strand(y_ref, c_ref, e_ref, s, g):
                entering = jnp.concatenate([in_ref[2 * j, s], in_ref[2 * j + 1, s]], 1)
                y = y_ref[:, lanes].astype(F32) + jnp.concatenate([dot(e_ref[0], s) for s in spreads], 0) * dot(
                    c_ref[...], entering
                )
                y = y * gate
                g[:, lanes] = y
                square = y * y
                return square[:, :128] + square[:, 128:]

            total_f = total_f + strand(yf_ref, cf_ref, ef_ref, 0, gf)
            total_b = total_b + strand(yb_ref, cb_ref, eb_ref, 1, gb)
        accf[...] = total_f
        accb[...] = total_b

    @pl.when(jnp.logical_not(worst <= LIMIT))
    def _():
        par[...] = jnp.zeros_like(par)
        for q in range(packs):
            par[0:1, q * heads : (q + 1) * heads] = decay_ref[...]
            par[1:2, q * heads : (q + 1) * heads] = skip_ref[...]
        accf[...] = jnp.zeros_like(accf)
        accb[...] = jnp.zeros_like(accb)
        for s, (x_any, s_any, g, acc) in enumerate(((xf_any, sf_any, gf, accf), (xb_any, sb_any, gb, accb))):
            keep = triangle(s == 0)
            ones = jnp.where(keep, 1.0, 0.0)

            def one_chunk(k, _):
                c = i * per_block + k
                copies = [
                    pltpu.make_async_copy(x_any.at[pl.ds(c * CHUNK, CHUNK)], xbuf, sem.at[0]),
                    pltpu.make_async_copy(s_any.at[c], sbuf, sem.at[1]),
                    pltpu.make_async_copy(step_any.at[group], dtbuf, sem.at[2]),
                ]
                for copy in copies:
                    copy.start()
                for copy in copies:
                    copy.wait()
                at = pl.ds(pl.multiple_of(k * CHUNK, CHUNK), CHUNK)
                dt = dtbuf[...]
                log_decay = jnp.dot(ones, -dt * par[0:1, :], precision=HIGHEST, preferred_element_type=F32)
                picked = iota(off_ref.shape, 0) == s * groups + group
                offset = jnp.sum(jnp.where(picked, off_ref[...], 0.0), 0, keepdims=True)
                log_t, dt_t = log_decay.T, dt.T
                b_part, c_part = xbuf[:, inner : inner + state], xbuf[:, inner + state :]
                scores = dot_nt(c_part, b_part)
                lane, sub = iota((CHUNK, 128), 1), iota((128, CHUNK), 0)
                lane1 = iota((1, 128), 1)
                left = lane < head_dim

                def pair(q, _):
                    cols = pl.ds(pl.multiple_of(q * 128, 128), 128)
                    v = xbuf[:, cols]
                    outs, ups, skips, offsets = [], [], [], []
                    for half in range(2):
                        h = 2 * q + half + (slot + k) * heads
                        column = jnp.sum(jnp.where(lane == h, log_decay, 0.0), 1, keepdims=True)
                        line = jnp.sum(jnp.where(sub == h, log_t, 0.0), 0, keepdims=True)
                        dt_line = jnp.sum(jnp.where(sub == h, dt_t, 0.0), 0, keepdims=True)
                        decay = jnp.where(keep, jnp.exp(jnp.minimum(column - line, 0.0)), 0.0)
                        outs.append(dot((decay * scores * dt_line).astype(BF16), v))
                        ups.append(jnp.exp(column))
                        skips.append(jnp.sum(jnp.where(lane1 == h, par[1:2, :], 0.0), 1, keepdims=True))
                        offsets.append(jnp.sum(jnp.where(lane1 == h, offset, 0.0), 1, keepdims=True))
                    shift = jnp.where(lane1 < head_dim, offsets[0], offsets[1])
                    entering = sbuf[:, cols].astype(F32) + jnp.exp(shift) * in_ref[q, s].astype(F32)
                    carried = dot(c_part, entering.astype(BF16))
                    y = jnp.where(left, outs[0], outs[1]) + jnp.where(left, ups[0], ups[1]) * carried
                    y = y + jnp.where(lane1 < head_dim, skips[0], skips[1]) * v.astype(F32)
                    y = y * silu(gate_ref[at, cols].astype(F32))
                    g[at, cols] = y
                    acc[at, :] += y * y
                    return 0

                lax.fori_loop(0, heads // 2, pair, 0)
                return 0

            lax.fori_loop(0, per_block, one_chunk, 0)

    scale_f = lax.rsqrt(jnp.sum(accf[...], 1, keepdims=True) * (1.0 / inner) + 1e-05)
    scale_b = lax.rsqrt(jnp.sum(accb[...], 1, keepdims=True) * (1.0 / inner) + 1e-05)
    order = shuffle(True)
    for j in range(inner // TILE):
        lanes = slice(j * TILE, (j + 1) * TILE)
        value = (gf[:, lanes] * scale_f + gb[:, lanes] * scale_b) * gain_ref[:, lanes]
        value = value.astype(BF16)
        for k in range(per_block):
            at = slice(k * CHUNK, (k + 1) * CHUNK)
            normed[at, lanes] = dot(order, value[at]).astype(BF16)
    out_ref[...] = (x_ref[...].astype(F32) + dot(normed[...], w_ref[...])).astype(BF16)


def local(hidden, in_weight, conv_weight, conv_bias, step_bias, decay_rate, skip_gain, norm_gain, out_weight):
    length, width = hidden.shape
    heads = step_bias.shape[0]
    inner = out_weight.shape[0]
    head_dim = inner // heads
    conv_width = conv_weight.shape[1]
    state = (conv_width - inner) // 2
    chunks = length // CHUNK
    tiles = inner // TILE
    count = lax.axis_size("ctx")
    groups = -(-chunks * heads // 128)
    ring = range(count)
    prev = lax.ppermute(hidden[length - HALO :], "ctx", [(i, i + 1) for i in ring if i + 1 < count])
    follow = lax.ppermute(hidden[:HALO], "ctx", [(i + 1, i) for i in ring if i + 1 < count])
    sizes = (heads, head_dim, state, inner)

    def whole(shape, **kw):
        return pl.BlockSpec(shape, lambda j: (0,) * len(shape), **kw)

    def value_tile(j):
        return jnp.clip(j - 1, 0, tiles - 1)

    def conv_tile(j):
        return jnp.where(j == 0, tiles, value_tile(j))

    def weight_tile(j):
        return jnp.where(j == 0, 2 * tiles, jnp.where(j <= tiles, tiles - 1 + j, j - tiles - 1))

    def shape(dims, dtype):
        return jax.ShapeDtypeStruct(dims, dtype)

    row2 = lambda a: a.reshape(1, -1)
    once = dict(pipeline_mode=pl.Buffered(1))
    outs = pl.pallas_call(
        functools.partial(front_kernel, *sizes),
        name="front",
        grid=(1 + 2 * tiles,),
        in_specs=[
            whole((length, width), **once),
            whole((HALO, width)),
            whole((HALO, width)),
            pl.BlockSpec((TILE, width), lambda j: (weight_tile(j), 0)),
            pl.BlockSpec((heads, width), lambda j: ((inner + conv_width) // heads, 0), **once),
            pl.BlockSpec((4, TILE), lambda j: (0, conv_tile(j))),
            pl.BlockSpec((1, TILE), lambda j: (0, conv_tile(j))),
            whole((1, heads)),
            whole((1, heads)),
            whole((1, heads)),
        ],
        out_specs=[
            pl.BlockSpec((length, TILE), lambda j: (0, jnp.maximum(j - tiles - 1, 0))),
            pl.BlockSpec((length, TILE), lambda j: (0, conv_tile(j))),
            pl.BlockSpec((length, TILE), lambda j: (0, conv_tile(j))),
            pl.BlockSpec((length, TILE), lambda j: (0, value_tile(j))),
            pl.BlockSpec((length, TILE), lambda j: (0, value_tile(j))),
            pl.BlockSpec((chunks, state, TILE), lambda j: (0, 0, value_tile(j))),
            pl.BlockSpec((chunks, state, TILE), lambda j: (0, 0, value_tile(j))),
            pl.BlockSpec((TILE // 128, 2, state + 16, 128), lambda j: (value_tile(j), 0, 0, 0)),
            whole((groups, CHUNK, 256)),
            whole((groups, CHUNK, 256)),
            whole((groups, CHUNK, 128)),
            whole((4 * groups, 128)),
            pl.BlockSpec(memory_space=pltpu.SMEM),
        ],
        out_shape=[
            shape((length, inner), BF16),
            shape((length, conv_width), BF16),
            shape((length, conv_width), BF16),
            shape((length, inner), BF16),
            shape((length, inner), BF16),
            shape((chunks, state, inner), BF16),
            shape((chunks, state, inner), BF16),
            shape((inner // 128, 2, state + 16, 128), BF16),
            shape((groups, CHUNK, 256), BF16),
            shape((groups, CHUNK, 256), BF16),
            shape((groups, CHUNK, 128), F32),
            shape((4 * groups, 128), F32),
            shape((groups,), F32),
        ],
        scratch_shapes=[
            pltpu.VMEM((length + 2 * HALO, width), BF16),
            pltpu.VMEM((chunks * (CHUNK + 48), TILE), F32),
            pltpu.VMEM((8, 128), F32),
        ]
        + [pltpu.VMEM((groups, CHUNK, 256), BF16)] * 4
        + [pltpu.VMEM((length, CHUNK + state), BF16)] * 2
        + [pltpu.VMEM((chunks * state, CHUNK), BF16)] * 2
        + [pltpu.VMEM((16, 128), BF16)]
        + [pltpu.VMEM((chunks, CHUNK + state, TILE), BF16)] * 2,
        compiler_params=pltpu.CompilerParams(vmem_limit_bytes=VMEM),
    )(
        hidden, follow, prev, in_weight.T, in_weight.T, conv_weight, row2(conv_bias), row2(step_bias), row2(decay_rate),
        row2(skip_gain),
    )
    gate, xf, xb, yf, yb, sf, sb, end, ef, eb, step, off, span = outs
    entering = pl.pallas_call(
        carry_kernel,
        name="carry",
        in_specs=[pl.BlockSpec(memory_space=pltpu.VMEM)],
        out_specs=pl.BlockSpec(memory_space=pltpu.VMEM),
        out_shape=shape((count, 2, state, 128), BF16),
        scratch_shapes=[
            pltpu.VMEM((count // 2, 2, state + 16, 128), BF16),
            pltpu.VMEM((count // 2, 2, state + 16, 128), BF16),
            pltpu.VMEM((count // 2, 2, state + 16, 128), BF16),
            pltpu.VMEM((count // 2, 2, state, 128), BF16),
            pltpu.VMEM((count // 2, 2, state, 128), BF16),
            pltpu.VMEM((count // 2, 2, state, 128), BF16),
        ]
        + [pltpu.SemaphoreType.DMA((count // 2,))] * 4
        + [pltpu.SemaphoreType.DMA((2,))] * 3,
        compiler_params=pltpu.CompilerParams(collective_id=0, has_side_effects=True, vmem_limit_bytes=VMEM),
    )(end)
    anywhere = pl.BlockSpec(memory_space=pl.ANY)
    block = pl.BlockSpec((ROWS, inner), lambda j: (j, 0))
    c_block = pl.BlockSpec((ROWS, state), lambda j: (j, inner // state + 1))
    e_block = pl.BlockSpec((1, CHUNK, 256), lambda j: (j * (ROWS // CHUNK) // (128 // heads), 0, 0))
    return pl.pallas_call(
        functools.partial(back_kernel, *sizes),
        name="back",
        grid=(length // ROWS,),
        in_specs=[
            pl.BlockSpec(memory_space=pltpu.SMEM),
            block, block, block, c_block, c_block, e_block, e_block,
            whole((count, 2, state, 128), **once),
            pl.BlockSpec((ROWS, width), lambda j: (j, 0)),
            whole((inner, width), **once),
            whole((1, inner)),
            whole((1, heads)),
            whole((1, heads)),
            whole((4 * groups, 128)),
        ]
        + [anywhere] * 5,
        out_specs=pl.BlockSpec((ROWS, width), lambda j: (j, 0)),
        out_shape=shape((length, width), BF16),
        scratch_shapes=[
            pltpu.VMEM((ROWS, inner), F32),
            pltpu.VMEM((ROWS, inner), F32),
            pltpu.VMEM((ROWS, 128), F32),
            pltpu.VMEM((ROWS, 128), F32),
            pltpu.VMEM((ROWS, inner), BF16),
            pltpu.VMEM((8, 128), F32),
            pltpu.VMEM((CHUNK, conv_width), BF16),
            pltpu.VMEM((state, inner), BF16),
            pltpu.VMEM((CHUNK, 128), F32),
            pltpu.SemaphoreType.DMA((3,)),
        ],
        compiler_params=pltpu.CompilerParams(vmem_limit_bytes=VMEM),
    )(
        span, yf, yb, gate, xf, xb, ef, eb, entering, hidden, out_weight, row2(norm_gain), row2(decay_rate),
        row2(skip_gain), off, xf, xb, sf, sb, step,
    )


def solution(mesh):
    return jax.shard_map(
        local,
        mesh=mesh,
        in_specs=(P(("dp", "ctx"), None), P(), P(), P(), P(), P(), P(), P(), P()),
        out_specs=P(("dp", "ctx"), None),
        check_vma=False,
    )
```

```python
import functools

import jax
import jax.numpy as jnp
from jax import lax
from jax.experimental import pallas as pl
from jax.experimental.pallas import tpu as pltpu
from jax.sharding import PartitionSpec as P

CHUNK = 128
TILE = 256
HALO = 8
ROWS = 256
LIMIT = 40.0
VMEM = 66_000_000
MESH = pl.DeviceIdType.MESH
HIGHEST = lax.Precision.HIGHEST
F32 = jnp.float32
BF16 = jnp.bfloat16


def dot(a, b):
    return jnp.dot(a, b, preferred_element_type=F32)


def dot_nt(a, b):
    return lax.dot_general(a, b, (((1,), (1,)), ((), ())), preferred_element_type=F32)


def silu(x):
    half = 0.5 * x
    return half + half * jnp.tanh(half)


def iota(shape, dim):
    return lax.broadcasted_iota(jnp.int32, shape, dim)


def iota_mod(shape, dim, mod):
    return lax.rem(iota(shape, dim), mod)


def time_of(index):
    return lax.rem(index, 8) * (CHUNK // 8) + lax.div(index, 8)


def triangle(lower):
    row, column = time_of(iota((CHUNK, CHUNK), 0)), time_of(iota((CHUNK, CHUNK), 1))
    return row >= column if lower else row <= column


def shuffle(inverse):
    row, column = iota((CHUNK, CHUNK), 0), iota((CHUNK, CHUNK), 1)
    hit = row == time_of(column) if inverse else time_of(row) == column
    return jnp.where(hit, 1.0, 0.0).astype(BF16)


def high_low(x):
    high = x.astype(BF16)
    return jnp.concatenate([high, (x - high.astype(F32)).astype(BF16)], 1)


def three_terms(x):
    high = x.astype(BF16).astype(F32)
    middle = (x - high).astype(BF16).astype(F32)
    return [high, middle, x - high - middle]


def spread_matrix(first, head_dim, depth):
    row, column = iota_mod((depth, TILE), 0, 128), iota((depth, TILE), 1)
    return jnp.where(row == first + lax.div(column, head_dim), 1.0, 0.0).astype(BF16)


def front_kernel(
    heads, head_dim, state, inner, x_ref, w_ref, wdt_ref, cw_ref, cb_ref, bias_ref, decay_ref, skip_ref,
    gate_ref, xf_ref, xb_ref, yf_ref, yb_ref, sf_ref, sb_ref, in_ref, ef_ref, eb_ref, step_ref, off_ref, span_ref,
    hx, xs, par, wf, wb, of, ob, gcf, gcb, btf, btb, small, rhs, kept_x, ends,
    follow, before_me, paired, chip, arrived, answers, entering, other, landed,
    halo_out, halo_in, pair_out, pair_in, first_out, first_in, second_out, second_in, back_out, back_in, own_sem,
):
    length = x_ref.shape[0]
    chunks = length // CHUNK
    tiles = inner // TILE
    packs = 128 // heads
    groups = off_ref.shape[0] // 4
    edge = 24
    span = CHUNK + 2 * edge
    j = pl.program_id(0)
    count = lax.axis_size("ctx")
    me = lax.axis_index("ctx")
    core, mine = lax.rem(me, 2), lax.div(me, 2)
    partner = me + 1 - 2 * core
    low = core == 0
    peers = count // 2
    chips = [lax.rem(mine + d, peers) for d in range(1, peers)]
    half_tiles = tiles // 2
    per_tile = TILE // 128

    def send(src, dst, out_sem, in_sem, peer):
        return pltpu.make_async_remote_copy(
            src_ref=src, dst_ref=dst, send_sem=out_sem, recv_sem=in_sem, device_id={"ctx": peer}, device_id_type=MESH
        )

    def halos():
        edge_rows = follow.shape[0]
        return [
            send(x_ref.at[:edge_rows], follow, halo_out.at[0], halo_in.at[0], lax.rem(me + count - 1, count)),
            send(
                x_ref.at[length - edge_rows :], before_me, halo_out.at[1], halo_in.at[1], lax.rem(me + 1, count)
            ),
        ]

    def pair_copy(t):
        at = pl.ds(t * per_tile, per_tile)
        slot = lax.rem(t, half_tiles)
        return send(
            ends.at[at], paired.at[pl.ds(slot * per_tile, per_tile)], pair_out.at[slot], pair_in.at[slot], partner
        )

    def total(ref, k):
        rows = ref[k, 0, state : state + 16, :].astype(F32)
        return rows[0:1] + rows[1:2] + rows[2:3]

    def first_copy(k):
        return send(chip.at[k], arrived.at[mine], first_out.at[k], first_in.at[mine], 2 * k + core)

    def combine(t):
        slot = lax.rem(t, half_tiles)
        pair_copy(t).wait_recv()
        for half in range(per_tile):
            k = slot * per_tile + half
            at = core * peers + k
            t_own, t_part = total(ends, at), total(paired, k)
            f_own, f_part = jnp.exp(t_own), jnp.exp(t_part)
            one = jnp.ones_like(f_own)
            own0, part0 = ends[at, 0, :state, :].astype(F32), paired[k, 0, :state, :].astype(F32)
            own1, part1 = ends[at, 1, :state, :].astype(F32), paired[k, 1, :state, :].astype(F32)
            chip[k, 0, :state, :] = (
                own0 * jnp.where(low, f_part, one) + part0 * jnp.where(low, one, f_own)
            ).astype(BF16)
            chip[k, 1, :state, :] = (
                own1 * jnp.where(low, one, f_part) + part1 * jnp.where(low, f_own, one)
            ).astype(BF16)
            extra = jnp.concatenate(three_terms(t_own + t_part) + [jnp.zeros((13, 128), F32)], 0).astype(BF16)
            chip[k, 0, state:, :] = extra
            chip[k, 1, state:, :] = extra

            @pl.when(k != mine)
            def _():
                first_copy(k).start()

            @pl.when(k == mine)
            def _():
                pltpu.make_async_copy(chip.at[k], arrived.at[k], own_sem.at[0]).start()

    def second_copy(k):
        return send(answers.at[k], entering.at[mine], second_out.at[k], second_in.at[mine], 2 * k + core)

    def scan():
        pltpu.make_async_copy(chip.at[mine], arrived.at[mine], own_sem.at[0]).wait()
        for k in chips:
            send(chip.at[k], arrived.at[k], first_out.at[k], first_in.at[k], 2 * k + core).wait_recv()
        for strand, order in ((0, list(range(peers))), (1, list(reversed(range(peers))))):
            running = jnp.zeros((state, 128), F32)
            for k in order:
                answers[k, strand] = running.astype(BF16)
                if k != order[-1]:
                    running = jnp.exp(total(arrived, k)) * running + arrived[k, strand, :state, :].astype(F32)
        for k in chips:
            second_copy(k).start()
        pltpu.make_async_copy(answers.at[mine], entering.at[mine], own_sem.at[1]).start()

    def back_copy():
        return send(other, landed, back_out.at[0], back_in.at[0], partner)

    def enter():
        pltpu.make_async_copy(answers.at[mine], entering.at[mine], own_sem.at[1]).wait()
        for k in chips:
            send(answers.at[k], entering.at[k], second_out.at[k], second_in.at[k], 2 * k + core).wait_recv()

        def one_pair(k, _):
            at = core * peers + k
            f_own, f_part = jnp.exp(total(ends, at)), jnp.exp(total(paired, k))
            chip_f, chip_b = entering[k, 0].astype(F32), entering[k, 1].astype(F32)
            own_late_f = f_part * chip_f + paired[k, 0, :state, :].astype(F32)
            part_late_f = f_own * chip_f + ends[at, 0, :state, :].astype(F32)
            own_late_b = f_part * chip_b + paired[k, 1, :state, :].astype(F32)
            part_late_b = f_own * chip_b + ends[at, 1, :state, :].astype(F32)
            in_ref[at, 0] = jnp.where(low, chip_f, own_late_f).astype(BF16)
            other[k, 0] = jnp.where(low, part_late_f, chip_f).astype(BF16)
            in_ref[at, 1] = jnp.where(low, own_late_b, chip_b).astype(BF16)
            other[k, 1] = jnp.where(low, chip_b, part_late_b).astype(BF16)
            return 0

        lax.fori_loop(0, peers, one_pair, 0)
        back_copy().start()

    def finish():
        back_copy().wait()

        def one_pair(k, _):
            in_ref[(1 - core) * peers + k] = landed[k]
            return 0

        lax.fori_loop(0, peers, one_pair, 0)
        for copy in halos():
            copy.wait_send()
        for slot in range(half_tiles):
            pair_copy((1 - core) * half_tiles + slot).wait_send()
        for k in chips:
            first_copy(k).wait_send()
            second_copy(k).wait_send()

    def project():
        out = dot_nt(hx[...], w_ref[...])
        for c in range(chunks):
            xs[c * span + edge : c * span + edge + CHUNK] = out[c * CHUNK : (c + 1) * CHUNK]
        sub = iota((8, TILE), 0)

        def rolled(c, r, by):
            at = c * span + edge + r * 8
            return pltpu.roll(xs[at : at + 8], by, 0)

        for p in range(3):
            r = CHUNK // 8 - 3 + p
            before = jnp.broadcast_to(out[length + 2 * HALO - 3 + p : length + 2 * HALO - 2 + p], (8, TILE))
            for c in range(chunks):
                mine = rolled(c, r, 1)
                xs[c * span + p * 8 : c * span + p * 8 + 8] = jnp.where(sub == 0, before, mine)
                before = mine
            after = jnp.broadcast_to(out[length + p : length + p + 1], (8, TILE))
            for c in reversed(range(chunks)):
                mine = rolled(c, p, 7)
                at = c * span + edge + CHUNK + p * 8
                xs[at : at + 8] = jnp.where(sub == 7, after, mine)
                after = mine

    def convolved(c):
        at = c * span + edge
        taps = [cw_ref[k : k + 1, :] for k in range(4)]
        base = xs[at : at + CHUNK] * taps[3] + cb_ref[...]
        forward, backward = base, base
        for k in range(1, 4):
            forward = forward + xs[at - 8 * k : at - 8 * k + CHUNK] * taps[3 - k]
            backward = backward + xs[at + 8 * k : at + 8 * k + CHUNK] * taps[3 - k]
        return silu(forward), silu(backward)

    @pl.when(j == 0)
    def _():
        barrier = pltpu.get_barrier_semaphore()
        beside = lax.rem(me + count - 1 + 2 * core, count)
        for peer in [partner, beside] + [2 * k + core for k in chips]:
            pl.semaphore_signal(barrier, inc=1, device_id={"ctx": peer}, device_id_type=MESH)
        pl.semaphore_wait(barrier, peers + 1)
        for copy in halos():
            copy.start()
        order = shuffle(False)
        for c in range(chunks):
            rows = slice(c * CHUNK, (c + 1) * CHUNK)
            hx[rows] = dot(order, x_ref[rows]).astype(BF16)
        par[...] = jnp.zeros_like(par)
        for q in range(packs):
            par[0:1, q * heads : (q + 1) * heads] = bias_ref[...]
            par[1:2, q * heads : (q + 1) * heads] = decay_ref[...]
        par[2:3, :heads] = skip_ref[...]
        lower = jnp.where(triangle(True), 1.0, 0.0)
        upper = jnp.where(triangle(False), 1.0, 0.0)
        lane1 = iota((1, 128), 1)
        wdt = wdt_ref[...]
        zero = jnp.zeros((128, wdt.shape[1]), BF16)
        totals, kept = [], []
        for g in range(groups):
            members = range(g * packs, min((g + 1) * packs, chunks))
            raw = jnp.zeros((CHUNK, 128), F32)
            for q, c in enumerate(members):
                parts = [zero[: q * heads], wdt, zero[: 128 - (q + 1) * heads]]
                wide = jnp.concatenate([p for p in parts if p.shape[0]], 0)
                raw = raw + dot_nt(hx[c * CHUNK : (c + 1) * CHUNK], wide)
            raw = raw.astype(BF16).astype(F32) + par[0:1, :]
            step = jnp.maximum(raw, 0.0) + jnp.log1p(jnp.exp(-jnp.abs(raw)))
            step = jnp.where(iota((CHUNK, 128), 1) < len(members) * heads, step, 0.0)
            step_ref[g] = step
            rate = -step * par[1:2, :]
            head = jnp.dot(lower, rate, precision=HIGHEST, preferred_element_type=F32)
            tail = jnp.dot(upper, rate, precision=HIGHEST, preferred_element_type=F32)
            total = head[CHUNK - 1 :]
            wf[g] = high_low(step * jnp.exp(jnp.minimum(total - head, 0.0)))
            wb[g] = high_low(step * jnp.exp(jnp.minimum(total - tail, 0.0)))
            of[g] = high_low(jnp.exp(jnp.minimum(head - total, 80.0)))
            ob[g] = high_low(jnp.exp(jnp.minimum(tail - total, 80.0)))
            totals.append(total)
            kept.append((head, tail))
            span_ref[g] = -jnp.min(total)

        def wide8(x):
            return jnp.broadcast_to(x, (8, 128))

        def both(x):
            w = wide8(x)
            for q in range(1, packs):
                w = w + pltpu.roll(wide8(x), q * heads, 1)
            return w[0:1]

        lane8 = iota((8, 128), 1)
        sums = [both(t) for t in totals]
        slab = sums[0]
        for t in sums[1:]:
            slab = slab + t
        for g in range(groups):
            t8 = wide8(totals[g])
            early, late = jnp.zeros((8, 128), F32), jnp.zeros((8, 128), F32)
            for q in range(1, packs):
                early = early + jnp.where(lane8 >= q * heads, pltpu.roll(t8, q * heads, 1), 0.0)
                late = late + jnp.where(lane8 < 128 - q * heads, pltpu.roll(t8, 128 - q * heads, 1), 0.0)
            early, late = early[0:1], late[0:1]
            for k in range(groups):
                if k < g:
                    early = early + sums[k]
                if k > g:
                    late = late + sums[k]
            off_ref[g : g + 1, :] = early
            off_ref[groups + g : groups + g + 1, :] = late
            off_ref[2 * groups + 2 * g : 2 * groups + 2 * g + 2, :] = jnp.zeros((2, 128), F32)
            ef_ref[g] = high_low(jnp.exp(kept[g][0] + early))
            eb_ref[g] = high_low(jnp.exp(kept[g][1] + late))
        lines = []
        for g in range(groups):
            lines += three_terms(jnp.exp(totals[g]))
        lines += three_terms(slab) + three_terms(par[2:3, :])
        lines.append(jnp.zeros((16 - len(lines), 128), F32))
        small[...] = jnp.concatenate(lines, 0).astype(BF16)
        for copy in halos():
            copy.wait_recv()
        first_row = jnp.where(me == count - 1, 0.0, 1.0)
        last_row = jnp.where(me == 0, 0.0, 1.0)
        hx[length:] = jnp.concatenate(
            [
                follow[...].astype(F32)[:HALO] * first_row,
                before_me[...].astype(F32)[before_me.shape[0] - HALO :] * last_row,
            ],
            0,
        ).astype(BF16)
        project()
        for c in range(chunks):
            rows = slice(c * CHUNK, (c + 1) * CHUNK)
            forward, backward = convolved(c)
            for value, out, gc, bt, keep in (
                (forward, xf_ref, gcf, btf, triangle(True)),
                (backward, xb_ref, gcb, btb, triangle(False)),
            ):
                rounded = value.astype(BF16)
                out[rows, :] = rounded
                b_part, c_part = rounded[:, :state], rounded[:, state:]
                gc[rows, :CHUNK] = jnp.where(keep, dot_nt(c_part, b_part), 0.0).astype(BF16)
                gc[rows, CHUNK:] = c_part
                bt[rows, :] = value[:, :state].T.astype(BF16)

    first = lax.rem(j - 1, tiles) * (TILE // head_dim)

    @pl.when((j >= 2) & (j <= tiles + 1) & (lax.div(j - 2, half_tiles) == core))
    def _():
        combine(j - 2)

    @pl.when(j == tiles + 1 + core * half_tiles)
    def _():
        scan()

    @pl.when((j == tiles + 1 + half_tiles) & low)
    def _():
        enter()

    @pl.when((j > 0) & (j <= tiles))
    def _():
        t = j - 1
        project()
        spreads = [spread_matrix(first + q * heads, head_dim, 256) for q in range(packs)]
        lines = [dot(small[...], spread[:128]) for spread in spreads]

        def line(q, k):
            rows = lines[q][3 * k : 3 * k + 3]
            return rows[0:1] + rows[1:2] + rows[2:3]

        fade = [line(c % packs, c // packs) for c in range(chunks)]
        slab = line(0, groups)
        for c in range(chunks):
            rows = slice(c * CHUNK, (c + 1) * CHUNK)
            g, spread = c // packs, spreads[c % packs]
            for strand, (value, x_out, w) in enumerate(zip(convolved(c), (xf_ref, xb_ref), (wf, wb))):
                rounded = value.astype(BF16)
                x_out[rows, :] = rounded
                kept_x[strand, t, rows] = rounded
                rhs[strand, t, c, :CHUNK] = (value * dot(w[g], spread)).astype(BF16)
        extra = jnp.concatenate(three_terms(slab) + [jnp.zeros((13, TILE), F32)], 0).astype(BF16)
        for strand, (order, s_ref, bt) in enumerate(
            ((range(chunks), sf_ref, btf), (reversed(range(chunks)), sb_ref, btb))
        ):
            running = jnp.zeros((state, TILE), F32)
            for c in order:
                rows = slice(c * CHUNK, (c + 1) * CHUNK)
                decayed = running * fade[c]
                s_ref[c] = running.astype(BF16)
                rhs[strand, t, c, CHUNK:] = decayed.astype(BF16)
                running = decayed + dot(bt[rows, :], rhs[strand, t, c, :CHUNK])
            for half in range(per_tile):
                lanes = slice(half * 128, (half + 1) * 128)
                ends[t * per_tile + half, strand, :state, :] = running[:, lanes].astype(BF16)
                ends[t * per_tile + half, strand, state:, :] = extra[:, lanes]

    @pl.when((j > 0) & (j <= tiles) & (lax.div(j - 1, half_tiles) != core))
    def _():
        pair_copy(j - 1).start()

    @pl.when(j > tiles)
    def _():
        t = j - 1 - tiles
        gate_ref[...] = dot_nt(hx[:length], w_ref[...]).astype(BF16)
        spreads = [spread_matrix(first + q * heads, head_dim, 256) for q in range(packs)]
        rows3 = dot(small[...], spreads[0][:128])[3 * groups + 3 : 3 * groups + 6]
        skip = rows3[0:1] + rows3[1:2] + rows3[2:3]
        for c in range(chunks):
            rows = slice(c * CHUNK, (c + 1) * CHUNK)
            g, spread = c // packs, spreads[c % packs]
            for strand, (y_ref, gc, o) in enumerate(((yf_ref, gcf, of), (yb_ref, gcb, ob))):
                mixed = dot(gc[rows, :], rhs[strand, t, c])
                y = mixed * dot(o[g], spread) + skip * kept_x[strand, t, rows].astype(F32)
                y_ref[rows, :] = y.astype(BF16)

    @pl.when(j == 2 * tiles)
    def _():
        @pl.when(jnp.logical_not(low))
        def _():
            enter()

        finish()


def back_kernel(
    heads, head_dim, state, inner, span_ref, yf_ref, yb_ref, gate_ref, cf_ref, cb_ref, ef_ref, eb_ref, in_ref, x_ref,
    w_ref, gain_ref, decay_ref, skip_ref, off_ref, xf_any, xb_any, sf_any, sb_any, step_any,
    out_ref, gf, gb, accf, accb, normed, par, xbuf, sbuf, dtbuf, sem,
):
    rows = out_ref.shape[0]
    i = pl.program_id(0)
    per_block = rows // CHUNK
    packs = 128 // heads
    groups = off_ref.shape[0] // 4
    group = lax.div(i * per_block, packs)
    slot = lax.rem(i * per_block, packs)
    worst = span_ref[group]

    @pl.when(worst <= LIMIT)
    def _():
        total_f = jnp.zeros((rows, 128), F32)
        total_b = jnp.zeros((rows, 128), F32)
        for j in range(inner // TILE):
            lanes = slice(j * TILE, (j + 1) * TILE)
            first = j * (TILE // head_dim)
            spreads = [spread_matrix(first + (slot + k) * heads, head_dim, 256) for k in range(per_block)]
            gate = silu(gate_ref[:, lanes].astype(F32))

            def strand(y_ref, c_ref, e_ref, s, g):
                entering = jnp.concatenate([in_ref[2 * j, s], in_ref[2 * j + 1, s]], 1)
                y = y_ref[:, lanes].astype(F32) + jnp.concatenate([dot(e_ref[0], s) for s in spreads], 0) * dot(
                    c_ref[...], entering
                )
                y = y * gate
                g[:, lanes] = y
                square = y * y
                return square[:, :128] + square[:, 128:]

            total_f = total_f + strand(yf_ref, cf_ref, ef_ref, 0, gf)
            total_b = total_b + strand(yb_ref, cb_ref, eb_ref, 1, gb)
        accf[...] = total_f
        accb[...] = total_b

    @pl.when(jnp.logical_not(worst <= LIMIT))
    def _():
        par[...] = jnp.zeros_like(par)
        for q in range(packs):
            par[0:1, q * heads : (q + 1) * heads] = decay_ref[...]
            par[1:2, q * heads : (q + 1) * heads] = skip_ref[...]
        accf[...] = jnp.zeros_like(accf)
        accb[...] = jnp.zeros_like(accb)
        for s, (x_any, s_any, g, acc) in enumerate(((xf_any, sf_any, gf, accf), (xb_any, sb_any, gb, accb))):
            keep = triangle(s == 0)
            ones = jnp.where(keep, 1.0, 0.0)

            def one_chunk(k, _):
                c = i * per_block + k
                copies = [
                    pltpu.make_async_copy(x_any.at[pl.ds(c * CHUNK, CHUNK)], xbuf, sem.at[0]),
                    pltpu.make_async_copy(s_any.at[c], sbuf, sem.at[1]),
                    pltpu.make_async_copy(step_any.at[group], dtbuf, sem.at[2]),
                ]
                for copy in copies:
                    copy.start()
                for copy in copies:
                    copy.wait()
                at = pl.ds(pl.multiple_of(k * CHUNK, CHUNK), CHUNK)
                dt = dtbuf[...]
                log_decay = jnp.dot(ones, -dt * par[0:1, :], precision=HIGHEST, preferred_element_type=F32)
                picked = iota(off_ref.shape, 0) == s * groups + group
                offset = jnp.sum(jnp.where(picked, off_ref[...], 0.0), 0, keepdims=True)
                log_t, dt_t = log_decay.T, dt.T
                b_part, c_part = xbuf[:, inner : inner + state], xbuf[:, inner + state :]
                scores = dot_nt(c_part, b_part)
                lane, sub = iota((CHUNK, 128), 1), iota((128, CHUNK), 0)
                lane1 = iota((1, 128), 1)
                left = lane < head_dim

                def pair(q, _):
                    cols = pl.ds(pl.multiple_of(q * 128, 128), 128)
                    v = xbuf[:, cols]
                    outs, ups, skips, offsets = [], [], [], []
                    for half in range(2):
                        h = 2 * q + half + (slot + k) * heads
                        column = jnp.sum(jnp.where(lane == h, log_decay, 0.0), 1, keepdims=True)
                        line = jnp.sum(jnp.where(sub == h, log_t, 0.0), 0, keepdims=True)
                        dt_line = jnp.sum(jnp.where(sub == h, dt_t, 0.0), 0, keepdims=True)
                        decay = jnp.where(keep, jnp.exp(jnp.minimum(column - line, 0.0)), 0.0)
                        outs.append(dot((decay * scores * dt_line).astype(BF16), v))
                        ups.append(jnp.exp(column))
                        skips.append(jnp.sum(jnp.where(lane1 == h, par[1:2, :], 0.0), 1, keepdims=True))
                        offsets.append(jnp.sum(jnp.where(lane1 == h, offset, 0.0), 1, keepdims=True))
                    shift = jnp.where(lane1 < head_dim, offsets[0], offsets[1])
                    entering = sbuf[:, cols].astype(F32) + jnp.exp(shift) * in_ref[q, s].astype(F32)
                    carried = dot(c_part, entering.astype(BF16))
                    y = jnp.where(left, outs[0], outs[1]) + jnp.where(left, ups[0], ups[1]) * carried
                    y = y + jnp.where(lane1 < head_dim, skips[0], skips[1]) * v.astype(F32)
                    y = y * silu(gate_ref[at, cols].astype(F32))
                    g[at, cols] = y
                    acc[at, :] += y * y
                    return 0

                lax.fori_loop(0, heads // 2, pair, 0)
                return 0

            lax.fori_loop(0, per_block, one_chunk, 0)

    scale_f = lax.rsqrt(jnp.sum(accf[...], 1, keepdims=True) * (1.0 / inner) + 1e-05)
    scale_b = lax.rsqrt(jnp.sum(accb[...], 1, keepdims=True) * (1.0 / inner) + 1e-05)
    order = shuffle(True)
    for j in range(inner // TILE):
        lanes = slice(j * TILE, (j + 1) * TILE)
        value = (gf[:, lanes] * scale_f + gb[:, lanes] * scale_b) * gain_ref[:, lanes]
        value = value.astype(BF16)
        for k in range(per_block):
            at = slice(k * CHUNK, (k + 1) * CHUNK)
            normed[at, lanes] = dot(order, value[at]).astype(BF16)
    out_ref[...] = (x_ref[...].astype(F32) + dot(normed[...], w_ref[...])).astype(BF16)


def local(hidden, in_weight, conv_weight, conv_bias, step_bias, decay_rate, skip_gain, norm_gain, out_weight):
    length, width = hidden.shape
    heads = step_bias.shape[0]
    inner = out_weight.shape[0]
    head_dim = inner // heads
    conv_width = conv_weight.shape[1]
    state = (conv_width - inner) // 2
    chunks = length // CHUNK
    tiles = inner // TILE
    count = lax.axis_size("ctx")
    groups = -(-chunks * heads // 128)
    sizes = (heads, head_dim, state, inner)

    def whole(shape, **kw):
        return pl.BlockSpec(shape, lambda j: (0,) * len(shape), **kw)

    def value_tile(j):
        return jnp.clip(j - 1, 0, tiles - 1)

    def conv_tile(j):
        return jnp.where(j == 0, tiles, value_tile(j))

    def weight_tile(j):
        return jnp.where(j == 0, 2 * tiles, jnp.where(j <= tiles, tiles - 1 + j, j - tiles - 1))

    def shape(dims, dtype):
        return jax.ShapeDtypeStruct(dims, dtype)

    row2 = lambda a: a.reshape(1, -1)
    once = dict(pipeline_mode=pl.Buffered(1))
    outs = pl.pallas_call(
        functools.partial(front_kernel, *sizes),
        name="front",
        grid=(1 + 2 * tiles,),
        in_specs=[
            whole((length, width), **once),
            pl.BlockSpec((TILE, width), lambda j: (weight_tile(j), 0)),
            pl.BlockSpec((heads, width), lambda j: ((inner + conv_width) // heads, 0), **once),
            pl.BlockSpec((4, TILE), lambda j: (0, conv_tile(j))),
            pl.BlockSpec((1, TILE), lambda j: (0, conv_tile(j))),
            whole((1, heads)),
            whole((1, heads)),
            whole((1, heads)),
        ],
        out_specs=[
            pl.BlockSpec((length, TILE), lambda j: (0, jnp.maximum(j - tiles - 1, 0))),
            pl.BlockSpec((length, TILE), lambda j: (0, conv_tile(j))),
            pl.BlockSpec((length, TILE), lambda j: (0, conv_tile(j))),
            pl.BlockSpec((length, TILE), lambda j: (0, jnp.maximum(j - tiles - 1, 0))),
            pl.BlockSpec((length, TILE), lambda j: (0, jnp.maximum(j - tiles - 1, 0))),
            pl.BlockSpec((chunks, state, TILE), lambda j: (0, 0, value_tile(j))),
            pl.BlockSpec((chunks, state, TILE), lambda j: (0, 0, value_tile(j))),
            whole((count, 2, state, 128)),
            whole((groups, CHUNK, 256)),
            whole((groups, CHUNK, 256)),
            whole((groups, CHUNK, 128)),
            whole((4 * groups, 128)),
            pl.BlockSpec(memory_space=pltpu.SMEM),
        ],
        out_shape=[
            shape((length, inner), BF16),
            shape((length, conv_width), BF16),
            shape((length, conv_width), BF16),
            shape((length, inner), BF16),
            shape((length, inner), BF16),
            shape((chunks, state, inner), BF16),
            shape((chunks, state, inner), BF16),
            shape((count, 2, state, 128), BF16),
            shape((groups, CHUNK, 256), BF16),
            shape((groups, CHUNK, 256), BF16),
            shape((groups, CHUNK, 128), F32),
            shape((4 * groups, 128), F32),
            shape((groups,), F32),
        ],
        scratch_shapes=[
            pltpu.VMEM((length + 2 * HALO, width), BF16),
            pltpu.VMEM((chunks * (CHUNK + 48), TILE), F32),
            pltpu.VMEM((8, 128), F32),
        ]
        + [pltpu.VMEM((groups, CHUNK, 256), BF16)] * 4
        + [pltpu.VMEM((length, CHUNK + state), BF16)] * 2
        + [pltpu.VMEM((chunks * state, CHUNK), BF16)] * 2
        + [pltpu.VMEM((16, 128), BF16)]
        + [
            pltpu.VMEM((2, tiles, chunks, CHUNK + state, TILE), BF16),
            pltpu.VMEM((2, tiles, length, TILE), BF16),
            pltpu.VMEM((count, 2, state + 16, 128), BF16),
            pltpu.VMEM((16, width), BF16),
            pltpu.VMEM((16, width), BF16),
        ]
        + [pltpu.VMEM((count // 2, 2, state + 16, 128), BF16)] * 3
        + [pltpu.VMEM((count // 2, 2, state, 128), BF16)] * 4
        + [pltpu.SemaphoreType.DMA((n,)) for n in (2, 2, tiles // 2, tiles // 2)]
        + [pltpu.SemaphoreType.DMA((count // 2,))] * 4
        + [pltpu.SemaphoreType.DMA((n,)) for n in (1, 1, 2)],
        compiler_params=pltpu.CompilerParams(collective_id=0, has_side_effects=True, vmem_limit_bytes=VMEM),
    )(
        hidden, in_weight.T, in_weight.T, conv_weight, row2(conv_bias), row2(step_bias), row2(decay_rate),
        row2(skip_gain),
    )
    gate, xf, xb, yf, yb, sf, sb, entering, ef, eb, step, off, span = outs
    anywhere = pl.BlockSpec(memory_space=pl.ANY)
    block = pl.BlockSpec((ROWS, inner), lambda j: (j, 0))
    c_block = pl.BlockSpec((ROWS, state), lambda j: (j, inner // state + 1))
    e_block = pl.BlockSpec((1, CHUNK, 256), lambda j: (j * (ROWS // CHUNK) // (128 // heads), 0, 0))
    return pl.pallas_call(
        functools.partial(back_kernel, *sizes),
        name="back",
        grid=(length // ROWS,),
        in_specs=[
            pl.BlockSpec(memory_space=pltpu.SMEM),
            block, block, block, c_block, c_block, e_block, e_block,
            whole((count, 2, state, 128), **once),
            pl.BlockSpec((ROWS, width), lambda j: (j, 0)),
            whole((inner, width), **once),
            whole((1, inner)),
            whole((1, heads)),
            whole((1, heads)),
            whole((4 * groups, 128)),
        ]
        + [anywhere] * 5,
        out_specs=pl.BlockSpec((ROWS, width), lambda j: (j, 0)),
        out_shape=shape((length, width), BF16),
        scratch_shapes=[
            pltpu.VMEM((ROWS, inner), F32),
            pltpu.VMEM((ROWS, inner), F32),
            pltpu.VMEM((ROWS, 128), F32),
            pltpu.VMEM((ROWS, 128), F32),
            pltpu.VMEM((ROWS, inner), BF16),
            pltpu.VMEM((8, 128), F32),
            pltpu.VMEM((CHUNK, conv_width), BF16),
            pltpu.VMEM((state, inner), BF16),
            pltpu.VMEM((CHUNK, 128), F32),
            pltpu.SemaphoreType.DMA((3,)),
        ],
        compiler_params=pltpu.CompilerParams(vmem_limit_bytes=VMEM),
    )(
        span, yf, yb, gate, xf, xb, ef, eb, entering, hidden, out_weight, row2(norm_gain), row2(decay_rate),
        row2(skip_gain), off, xf, xb, sf, sb, step,
    )


def solution(mesh):
    return jax.shard_map(
        local,
        mesh=mesh,
        in_specs=(P(("dp", "ctx"), None), P(), P(), P(), P(), P(), P(), P(), P()),
        out_specs=P(("dp", "ctx"), None),
        check_vma=False,
    )
```

```python
import functools

import jax
import jax.numpy as jnp
from jax import lax
from jax.experimental import pallas as pl
from jax.experimental.pallas import tpu as pltpu
from jax.sharding import PartitionSpec as P

CHUNK = 128
TILE = 256
HALO = 8
ROWS = 256
LIMIT = 40.0
VMEM = 66_000_000
MESH = pl.DeviceIdType.MESH
HIGHEST = lax.Precision.HIGHEST
F32 = jnp.float32
BF16 = jnp.bfloat16


def dot(a, b):
    return jnp.dot(a, b, preferred_element_type=F32)


def dot_nt(a, b):
    return lax.dot_general(a, b, (((1,), (1,)), ((), ())), preferred_element_type=F32)


def silu_of_half(half):
    return half + half * jnp.tanh(half)


def silu(x):
    return silu_of_half(0.5 * x)


def iota(shape, dim):
    return lax.broadcasted_iota(jnp.int32, shape, dim)


def iota_mod(shape, dim, mod):
    return lax.rem(iota(shape, dim), mod)


def time_of(index):
    return lax.rem(index, 8) * (CHUNK // 8) + lax.div(index, 8)


def triangle(lower):
    row, column = time_of(iota((CHUNK, CHUNK), 0)), time_of(iota((CHUNK, CHUNK), 1))
    return row >= column if lower else row <= column


def high_low(x):
    high = x.astype(BF16)
    return jnp.concatenate([high, (x - high.astype(F32)).astype(BF16)], 1)


def three_terms(x):
    high = x.astype(BF16).astype(F32)
    middle = (x - high).astype(BF16).astype(F32)
    return [high, middle, x - high - middle]


def spread_matrix(first, head_dim):
    row, column = iota((128, TILE), 0), iota((128, TILE), 1)
    half = jnp.where(row == first + lax.div(column, head_dim), 1.0, 0.0).astype(BF16)
    return jnp.concatenate([half, half], 0)


def front_kernel(
    heads, head_dim, state, inner, x_ref, w_ref, wbc_ref, wdt_ref, cw_ref, cb_ref, bias_ref, decay_ref, skip_ref,
    gate_ref, xf_ref, xb_ref, yf_ref, yb_ref, gf_ref, gb_ref, sf_ref, sb_ref, in_ref, step_ref, off_ref, span_ref,
    hx, xs0, xs1, gate0, gate1, par, wf, wb, of, ob, update, gcf, gcb, btf, btb, small, rhs, kept_x, ends,
    follow, before_me, paired, chip, arrived, answers, entering, other, landed,
    halo_out, halo_in, pair_out, pair_in, first_out, first_in, second_out, second_in, back_out, back_in, own_sem,
):
    length = x_ref.shape[0]
    chunks = length // CHUNK
    tiles = inner // TILE
    packs = 128 // heads
    groups = off_ref.shape[0] // 4
    edge = 24
    span = CHUNK + 2 * edge
    j = pl.program_id(0)
    count = lax.axis_size("ctx")
    me = lax.axis_index("ctx")
    core, mine = lax.rem(me, 2), lax.div(me, 2)
    partner = me + 1 - 2 * core
    low = core == 0
    peers = count // 2
    chips = [lax.rem(mine + d, peers) for d in range(1, peers)]
    half_tiles = tiles // 2
    per_tile = TILE // 128

    def send(src, dst, out_sem, in_sem, peer):
        return pltpu.make_async_remote_copy(
            src_ref=src, dst_ref=dst, send_sem=out_sem, recv_sem=in_sem, device_id={"ctx": peer}, device_id_type=MESH
        )

    def halos():
        edge_rows = follow.shape[0]
        return [
            send(x_ref.at[:edge_rows], follow, halo_out.at[0], halo_in.at[0], lax.rem(me + count - 1, count)),
            send(
                x_ref.at[length - edge_rows :], before_me, halo_out.at[1], halo_in.at[1], lax.rem(me + 1, count)
            ),
        ]

    def pair_copy(t):
        at = pl.ds(t * per_tile, per_tile)
        slot = lax.rem(t, half_tiles)
        return send(
            ends.at[at], paired.at[pl.ds(slot * per_tile, per_tile)], pair_out.at[slot], pair_in.at[slot], partner
        )

    def total(ref, k):
        rows = ref[k, 0, state : state + 16, :].astype(F32)
        return rows[0:1] + rows[1:2] + rows[2:3]

    def first_copy(k):
        return send(chip.at[k], arrived.at[mine], first_out.at[k], first_in.at[mine], 2 * k + core)

    def combine(t):
        slot = lax.rem(t, half_tiles)
        pair_copy(t).wait_recv()
        for half in range(per_tile):
            k = slot * per_tile + half
            at = core * peers + k
            t_own, t_part = total(ends, at), total(paired, k)
            f_own, f_part = jnp.exp(t_own), jnp.exp(t_part)
            one = jnp.ones_like(f_own)
            own0, part0 = ends[at, 0, :state, :].astype(F32), paired[k, 0, :state, :].astype(F32)
            own1, part1 = ends[at, 1, :state, :].astype(F32), paired[k, 1, :state, :].astype(F32)
            chip[k, 0, :state, :] = (
                own0 * jnp.where(low, f_part, one) + part0 * jnp.where(low, one, f_own)
            ).astype(BF16)
            chip[k, 1, :state, :] = (
                own1 * jnp.where(low, one, f_part) + part1 * jnp.where(low, f_own, one)
            ).astype(BF16)
            extra = jnp.concatenate(three_terms(t_own + t_part) + [jnp.zeros((13, 128), F32)], 0).astype(BF16)
            chip[k, 0, state:, :] = extra
            chip[k, 1, state:, :] = extra

            @pl.when(k != mine)
            def _():
                first_copy(k).start()

            @pl.when(k == mine)
            def _():
                pltpu.make_async_copy(chip.at[k], arrived.at[k], own_sem.at[0]).start()

    def second_copy(k):
        return send(answers.at[k], entering.at[mine], second_out.at[k], second_in.at[mine], 2 * k + core)

    def scan():
        pltpu.make_async_copy(chip.at[mine], arrived.at[mine], own_sem.at[0]).wait()
        for k in chips:
            send(chip.at[k], arrived.at[k], first_out.at[k], first_in.at[k], 2 * k + core).wait_recv()
        for strand, order in ((0, list(range(peers))), (1, list(reversed(range(peers))))):
            running = jnp.zeros((state, 128), F32)
            for k in order:
                answers[k, strand] = running.astype(BF16)
                if k != order[-1]:
                    running = jnp.exp(total(arrived, k)) * running + arrived[k, strand, :state, :].astype(F32)
        for k in chips:
            second_copy(k).start()
        pltpu.make_async_copy(answers.at[mine], entering.at[mine], own_sem.at[1]).start()

    def back_copy(k):
        return send(other.at[k], landed.at[k], back_out.at[k], back_in.at[k], partner)

    def enter():
        pltpu.make_async_copy(answers.at[mine], entering.at[mine], own_sem.at[1]).wait()

        def one_pair(d, _):
            k = lax.rem(mine + d, peers)

            @pl.when(d > 0)
            def _():
                send(answers.at[k], entering.at[k], second_out.at[k], second_in.at[k], 2 * k + core).wait_recv()

            at = core * peers + k
            f_own, f_part = jnp.exp(total(ends, at)), jnp.exp(total(paired, k))
            one, none = jnp.ones_like(f_own), jnp.zeros_like(f_own)
            for strand, early in ((0, low), (1, jnp.logical_not(low))):
                chip_in = entering[k, strand].astype(F32)
                scale, add = jnp.where(early, one, f_part), jnp.where(early, none, one)
                in_ref[at, strand] = (scale * chip_in + add * paired[k, strand, :state, :].astype(F32)).astype(BF16)
                scale, add = jnp.where(early, f_own, one), jnp.where(early, one, none)
                other[k, strand] = (scale * chip_in + add * ends[at, strand, :state, :].astype(F32)).astype(BF16)
            back_copy(k).start()
            return 0

        lax.fori_loop(0, peers, one_pair, 0)

    def finish():
        def one_pair(k, _):
            back_copy(k).wait()
            in_ref[(1 - core) * peers + k] = landed[k]
            return 0

        lax.fori_loop(0, peers, one_pair, 0)
        for copy in halos():
            copy.wait_send()
        for slot in range(half_tiles):
            pair_copy((1 - core) * half_tiles + slot).wait_send()
        for k in chips:
            first_copy(k).wait_send()
            second_copy(k).wait_send()

    def keep_rows(xs, out):
        for c in range(chunks):
            xs[c * span + edge : c * span + edge + CHUNK] = out[c * CHUNK : (c + 1) * CHUNK]

    def project(weights, xs):
        out = dot_nt(hx[...], weights[...])
        keep_rows(xs, out)
        join(xs, out[length:])

    def join(xs, out):
        sub = iota((8, TILE), 0)

        def rolled(c, r, by):
            at = c * span + edge + r * 8
            return pltpu.roll(xs[at : at + 8], by, 0)

        for p in range(3):
            r = CHUNK // 8 - 3 + p
            before = jnp.broadcast_to(out[2 * HALO - 3 + p : 2 * HALO - 2 + p], (8, TILE))
            for c in range(chunks):
                mine = rolled(c, r, 1)
                xs[c * span + p * 8 : c * span + p * 8 + 8] = jnp.where(sub == 0, before, mine)
                before = mine
            after = jnp.broadcast_to(out[p : p + 1], (8, TILE))
            for c in reversed(range(chunks)):
                mine = rolled(c, p, 7)
                at = c * span + edge + CHUNK + p * 8
                xs[at : at + 8] = jnp.where(sub == 7, after, mine)
                after = mine

    def convolved(xs, c):
        at = c * span + edge
        taps = [0.5 * cw_ref[k : k + 1, :] for k in range(4)]
        base = xs[at : at + CHUNK] * taps[3] + 0.5 * cb_ref[...]
        forward, backward = base, base
        for k in range(1, 4):
            forward = forward + xs[at - 8 * k : at - 8 * k + CHUNK] * taps[3 - k]
            backward = backward + xs[at + 8 * k : at + 8 * k + CHUNK] * taps[3 - k]
        return silu_of_half(forward), silu_of_half(backward)

    @pl.when(j == 0)
    def _():
        barrier = pltpu.get_barrier_semaphore()
        beside = lax.rem(me + count - 1 + 2 * core, count)
        for peer in [partner, beside] + [2 * k + core for k in chips]:
            pl.semaphore_signal(barrier, inc=1, device_id={"ctx": peer}, device_id_type=MESH)
        pl.semaphore_wait(barrier, peers + 1)
        for copy in halos():
            copy.start()
        order = jnp.where(time_of(iota((CHUNK, CHUNK), 0)) == iota((CHUNK, CHUNK), 1), 1.0, 0.0).astype(BF16)
        for c in range(chunks):
            rows = slice(c * CHUNK, (c + 1) * CHUNK)
            hx[rows] = dot(order, x_ref[rows]).astype(BF16)
        par[...] = jnp.zeros_like(par)
        for q in range(packs):
            par[0:1, q * heads : (q + 1) * heads] = bias_ref[...]
            par[1:2, q * heads : (q + 1) * heads] = decay_ref[...]
        par[2:3, :heads] = skip_ref[...]
        lower = jnp.where(triangle(True), 1.0, 0.0)
        upper = jnp.where(triangle(False), 1.0, 0.0)
        lane1 = iota((1, 128), 1)
        wdt = jnp.concatenate([wdt_ref[...], jnp.zeros((128 - heads, wdt_ref.shape[1]), BF16)], 0)
        all_raw = dot_nt(hx[:length], wdt)
        keep_rows(xs1, dot_nt(hx[:length], wbc_ref[...]))
        totals = []
        for g in range(groups):
            members = range(g * packs, min((g + 1) * packs, chunks))
            raw = jnp.zeros((CHUNK, 128), F32)
            for q, c in enumerate(members):
                one = all_raw[c * CHUNK : (c + 1) * CHUNK]
                raw = raw + (pltpu.roll(one, q * heads, 1) if q else one)
            raw = raw.astype(BF16).astype(F32) + par[0:1, :]
            step = jnp.maximum(raw, 0.0) + jnp.log1p(jnp.exp(-jnp.abs(raw)))
            step = jnp.where(iota((CHUNK, 128), 1) < len(members) * heads, step, 0.0)
            step_ref[g] = step
            rate = -step * par[1:2, :]
            head = jnp.dot(lower, rate, precision=HIGHEST, preferred_element_type=F32)
            tail = jnp.dot(upper, rate, precision=HIGHEST, preferred_element_type=F32)
            total = head[CHUNK - 1 :]
            wf[g] = high_low(step * jnp.exp(jnp.minimum(total - head, 0.0)))
            wb[g] = high_low(step * jnp.exp(jnp.minimum(total - tail, 0.0)))
            of[g] = high_low(jnp.exp(jnp.minimum(head - total, 80.0)))
            ob[g] = high_low(jnp.exp(jnp.minimum(tail - total, 80.0)))
            totals.append(total)
            span_ref[g] = -jnp.min(total)

        def wide8(x):
            return jnp.broadcast_to(x, (8, 128))

        def both(x):
            w = wide8(x)
            for q in range(1, packs):
                w = w + pltpu.roll(wide8(x), q * heads, 1)
            return w[0:1]

        lane8 = iota((8, 128), 1)
        sums = [both(t) for t in totals]
        slab = sums[0]
        for t in sums[1:]:
            slab = slab + t
        reach = []
        for g in range(groups):
            t8 = wide8(totals[g])
            early, late = jnp.zeros((8, 128), F32), jnp.zeros((8, 128), F32)
            for q in range(1, packs):
                early = early + jnp.where(lane8 >= q * heads, pltpu.roll(t8, q * heads, 1), 0.0)
                late = late + jnp.where(lane8 < 128 - q * heads, pltpu.roll(t8, 128 - q * heads, 1), 0.0)
            early, late = early[0:1], late[0:1]
            for k in range(groups):
                if k < g:
                    early = early + sums[k]
                if k > g:
                    late = late + sums[k]
            off_ref[g : g + 1, :] = early
            off_ref[groups + g : groups + g + 1, :] = late
            off_ref[2 * groups + 2 * g : 2 * groups + 2 * g + 2, :] = jnp.zeros((2, 128), F32)
            reach.append((jnp.exp(early + totals[g]), jnp.exp(late + totals[g])))
        lines = []
        for g in range(groups):
            lines += three_terms(jnp.exp(totals[g]))
        lines += three_terms(slab) + three_terms(par[2:3, :])
        for strand in range(2):
            for g in range(groups):
                lines += three_terms(reach[g][strand])
        lines.append(jnp.zeros((small.shape[0] - len(lines), 128), F32))
        small[...] = jnp.concatenate(lines, 0).astype(BF16)
        for copy in halos():
            copy.wait_recv()
        first_row = jnp.where(me == count - 1, 0.0, 1.0)
        last_row = jnp.where(me == 0, 0.0, 1.0)
        hx[length:] = jnp.concatenate(
            [
                follow[...].astype(F32)[:HALO] * first_row,
                before_me[...].astype(F32)[before_me.shape[0] - HALO :] * last_row,
            ],
            0,
        ).astype(BF16)
        join(xs1, dot_nt(hx[length:], wbc_ref[...]))
        for c in range(chunks):
            rows = slice(c * CHUNK, (c + 1) * CHUNK)
            forward, backward = convolved(xs1, c)
            for value, out, gc, bt, keep in (
                (forward, xf_ref, gcf, btf, triangle(True)),
                (backward, xb_ref, gcb, btb, triangle(False)),
            ):
                rounded = value.astype(BF16)
                out[rows, :] = rounded
                b_part, c_part = rounded[:, :state], rounded[:, state:]
                gc[rows, :CHUNK] = jnp.where(keep, dot_nt(c_part, b_part), 0.0).astype(BF16)
                gc[rows, CHUNK:] = c_part
                bt[rows, :] = value[:, :state].T.astype(BF16)
        project(w_ref, xs0)

    first = lax.rem(j - 1, tiles) * (TILE // head_dim)

    @pl.when((j >= 2) & (j <= tiles + 1) & (lax.div(j - 2, half_tiles) == core))
    def _():
        combine(j - 2)

    @pl.when(j == tiles + 1 + core * half_tiles)
    def _():
        scan()

    @pl.when((j == tiles + 1 + half_tiles) & low)
    def _():
        enter()

    def line_of(lines, q, k):
        rows = lines[q][3 * k : 3 * k + 3]
        return rows[0:1] + rows[1:2] + rows[2:3]

    def gating(gate):
        gate[...] = dot_nt(hx[:length], w_ref[...])

    def values_step(xs):
        t = j - 1
        spreads = [spread_matrix(first + q * heads, head_dim) for q in range(packs)]
        lines = [dot(small[...], spread[:128]) for spread in spreads]
        fade = [line_of(lines, c % packs, c // packs) for c in range(chunks)]
        slab = line_of(lines, 0, groups)

        def summarise(c, pair):
            for strand, (bt, scaled) in enumerate(zip((btf, btb), pair)):
                update[strand, c] = dot(bt[c * CHUNK : (c + 1) * CHUNK, :], scaled)

        scaled = None
        for c in range(chunks):
            rows = slice(c * CHUNK, (c + 1) * CHUNK)
            weights = [dot(w[c // packs], spreads[c % packs]) for w in (wf, wb)]
            if scaled is not None:
                summarise(c - 1, scaled)
            scaled = []
            for strand, (value, x_out) in enumerate(zip(convolved(xs, c), (xf_ref, xb_ref))):
                rounded = value.astype(BF16)
                x_out[rows, :] = rounded
                kept_x[strand, t, rows] = rounded
                scaled.append((value * weights[strand]).astype(BF16))
                rhs[strand, t, c, :CHUNK] = scaled[strand]
        summarise(chunks - 1, scaled)
        extra = jnp.concatenate(three_terms(slab) + [jnp.zeros((13, TILE), F32)], 0).astype(BF16)
        for strand, (order, s_ref) in enumerate(((range(chunks), sf_ref), (reversed(range(chunks)), sb_ref))):
            running = jnp.zeros((state, TILE), F32)
            for c in order:
                decayed = running * fade[c]
                s_ref[c] = running.astype(BF16)
                rhs[strand, t, c, CHUNK:] = decayed.astype(BF16)
                running = decayed + update[strand, c]
            for half in range(per_tile):
                lanes = slice(half * 128, (half + 1) * 128)
                ends[t * per_tile + half, strand, :state, :] = running[:, lanes].astype(BF16)
                ends[t * per_tile + half, strand, state:, :] = extra[:, lanes]

    @pl.when((j > 0) & (j < tiles) & (lax.rem(j, 2) == 1))
    def _():
        project(w_ref, xs1)
        values_step(xs0)

    @pl.when((j > 0) & (j < tiles) & (lax.rem(j, 2) == 0))
    def _():
        project(w_ref, xs0)
        values_step(xs1)

    @pl.when(j == tiles)
    def _():
        gating(gate0)
        values_step(xs1)

    @pl.when((j > 0) & (j <= tiles) & (lax.div(j - 1, half_tiles) != core))
    def _():
        pair_copy(j - 1).start()

    def outputs_step(gate):
        t = j - 1 - tiles
        spreads = [spread_matrix(first + q * heads, head_dim) for q in range(packs)]
        lines = [dot(small[...], spread[:128]) for spread in spreads]
        skip = line_of(lines, 0, groups + 1)
        for c in range(chunks):
            rows = slice(c * CHUNK, (c + 1) * CHUNK)
            raw = gate[rows]
            gate_ref[rows, :] = raw.astype(BF16)
            open_gate = silu(raw)
            for strand, (y_ref, g_ref, gc, o) in enumerate(
                ((yf_ref, gf_ref, gcf, of), (yb_ref, gb_ref, gcb, ob))
            ):
                scale = dot(o[c // packs], spreads[c % packs]) * open_gate
                mixed = dot(gc[rows, :], rhs[strand, t, c])
                y = mixed * scale + (skip * open_gate) * kept_x[strand, t, rows].astype(F32)
                y_ref[rows, :] = y.astype(BF16)
                reach = line_of(lines, c % packs, (strand + 1) * groups + 2 + c // packs)
                g_ref[rows, :] = (scale * reach).astype(BF16)

    @pl.when((j > tiles) & (j < 2 * tiles) & (lax.rem(j, 2) == 1))
    def _():
        gating(gate1)
        outputs_step(gate0)

    @pl.when((j > tiles) & (j < 2 * tiles) & (lax.rem(j, 2) == 0))
    def _():
        gating(gate0)
        outputs_step(gate1)

    @pl.when(j == 2 * tiles)
    def _():
        outputs_step(gate1)

    @pl.when(j == 2 * tiles)
    def _():
        @pl.when(jnp.logical_not(low))
        def _():
            enter()

        finish()


def back_kernel(
    heads, head_dim, state, inner, span_ref, yf_ref, yb_ref, gf_ref, gb_ref, cf_ref, cb_ref, in_ref, x_ref,
    w_ref, gain_ref, decay_ref, skip_ref, off_ref, gate_any, xf_any, xb_any, sf_any, sb_any, step_any,
    out_ref, gf, gb, accf, accb, normed, unshuffled, par, xbuf, sbuf, dtbuf, gatebuf, sem,
):
    rows = out_ref.shape[0]
    i = pl.program_id(0)
    per_block = rows // CHUNK
    packs = 128 // heads
    groups = off_ref.shape[0] // 4
    group = lax.div(i * per_block, packs)
    slot = lax.rem(i * per_block, packs)
    worst = span_ref[group]

    @pl.when(worst <= LIMIT)
    def _():
        total_f = jnp.zeros((rows, 128), F32)
        total_b = jnp.zeros((rows, 128), F32)
        for j in range(inner // TILE):
            lanes = slice(j * TILE, (j + 1) * TILE)

            def strand(y_ref, c_ref, g_ref, s, g):
                entering = jnp.concatenate([in_ref[2 * j, s], in_ref[2 * j + 1, s]], 1)
                y = y_ref[:, lanes].astype(F32) + g_ref[:, lanes].astype(F32) * dot(c_ref[...], entering)
                g[:, lanes] = y
                square = y * y
                return square[:, :128] + square[:, 128:]

            total_f = total_f + strand(yf_ref, cf_ref, gf_ref, 0, gf)
            total_b = total_b + strand(yb_ref, cb_ref, gb_ref, 1, gb)
        accf[...] = total_f
        accb[...] = total_b

    @pl.when(jnp.logical_not(worst <= LIMIT))
    def _():
        par[...] = jnp.zeros_like(par)
        for q in range(packs):
            par[0:1, q * heads : (q + 1) * heads] = decay_ref[...]
            par[1:2, q * heads : (q + 1) * heads] = skip_ref[...]
        accf[...] = jnp.zeros_like(accf)
        accb[...] = jnp.zeros_like(accb)
        for s, (x_any, s_any, g, acc) in enumerate(((xf_any, sf_any, gf, accf), (xb_any, sb_any, gb, accb))):
            keep = triangle(s == 0)
            ones = jnp.where(keep, 1.0, 0.0)

            def one_chunk(k, _):
                c = i * per_block + k
                copies = [
                    pltpu.make_async_copy(x_any.at[pl.ds(c * CHUNK, CHUNK)], xbuf, sem.at[0]),
                    pltpu.make_async_copy(s_any.at[c], sbuf, sem.at[1]),
                    pltpu.make_async_copy(step_any.at[group], dtbuf, sem.at[2]),
                    pltpu.make_async_copy(gate_any.at[pl.ds(c * CHUNK, CHUNK)], gatebuf, sem.at[3]),
                ]
                for copy in copies:
                    copy.start()
                for copy in copies:
                    copy.wait()
                at = pl.ds(pl.multiple_of(k * CHUNK, CHUNK), CHUNK)
                dt = dtbuf[...]
                log_decay = jnp.dot(ones, -dt * par[0:1, :], precision=HIGHEST, preferred_element_type=F32)
                picked = iota(off_ref.shape, 0) == s * groups + group
                offset = jnp.sum(jnp.where(picked, off_ref[...], 0.0), 0, keepdims=True)
                log_t, dt_t = log_decay.T, dt.T
                b_part, c_part = xbuf[:, inner : inner + state], xbuf[:, inner + state :]
                scores = dot_nt(c_part, b_part)
                lane, sub = iota((CHUNK, 128), 1), iota((128, CHUNK), 0)
                lane1 = iota((1, 128), 1)
                left = lane < head_dim

                def pair(q, _):
                    cols = pl.ds(pl.multiple_of(q * 128, 128), 128)
                    v = xbuf[:, cols]
                    outs, ups, skips, offsets = [], [], [], []
                    for half in range(2):
                        h = 2 * q + half + (slot + k) * heads
                        column = jnp.sum(jnp.where(lane == h, log_decay, 0.0), 1, keepdims=True)
                        line = jnp.sum(jnp.where(sub == h, log_t, 0.0), 0, keepdims=True)
                        dt_line = jnp.sum(jnp.where(sub == h, dt_t, 0.0), 0, keepdims=True)
                        decay = jnp.where(keep, jnp.exp(jnp.minimum(column - line, 0.0)), 0.0)
                        outs.append(dot((decay * scores * dt_line).astype(BF16), v))
                        ups.append(jnp.exp(column))
                        skips.append(jnp.sum(jnp.where(lane1 == h, par[1:2, :], 0.0), 1, keepdims=True))
                        offsets.append(jnp.sum(jnp.where(lane1 == h, offset, 0.0), 1, keepdims=True))
                    shift = jnp.where(lane1 < head_dim, offsets[0], offsets[1])
                    entering = sbuf[:, cols].astype(F32) + jnp.exp(shift) * in_ref[q, s].astype(F32)
                    carried = dot(c_part, entering.astype(BF16))
                    y = jnp.where(left, outs[0], outs[1]) + jnp.where(left, ups[0], ups[1]) * carried
                    y = y + jnp.where(lane1 < head_dim, skips[0], skips[1]) * v.astype(F32)
                    y = y * silu(gatebuf[:, cols].astype(F32))
                    g[at, cols] = y
                    acc[at, :] += y * y
                    return 0

                lax.fori_loop(0, heads // 2, pair, 0)
                return 0

            lax.fori_loop(0, per_block, one_chunk, 0)

    scale_f = lax.rsqrt(jnp.sum(accf[...], 1, keepdims=True) * (1.0 / inner) + 1e-05)
    scale_b = lax.rsqrt(jnp.sum(accb[...], 1, keepdims=True) * (1.0 / inner) + 1e-05)
    for j in range(inner // TILE):
        lanes = slice(j * TILE, (j + 1) * TILE)
        value = (gf[:, lanes] * scale_f + gb[:, lanes] * scale_b) * gain_ref[:, lanes]
        normed[:, lanes] = value.astype(BF16)
    steps = CHUNK // 8
    product = dot(normed[...], w_ref[...])
    for n in range(w_ref.shape[1] // 128):
        lanes = slice(n * 128, (n + 1) * 128)
        for k in range(per_block):
            for r in range(steps):
                at = k * CHUNK + r * 8
                unshuffled[n, pl.ds(k * CHUNK + r, 8, stride=steps), :] = product[at : at + 8, lanes]
        out_ref[:, lanes] = (x_ref[:, lanes].astype(F32) + unshuffled[n]).astype(BF16)


def local(hidden, in_weight, conv_weight, conv_bias, step_bias, decay_rate, skip_gain, norm_gain, out_weight):
    length, width = hidden.shape
    heads = step_bias.shape[0]
    inner = out_weight.shape[0]
    head_dim = inner // heads
    conv_width = conv_weight.shape[1]
    state = (conv_width - inner) // 2
    chunks = length // CHUNK
    tiles = inner // TILE
    count = lax.axis_size("ctx")
    groups = -(-chunks * heads // 128)
    sizes = (heads, head_dim, state, inner)

    def whole(shape, **kw):
        return pl.BlockSpec(shape, lambda j: (0,) * len(shape), **kw)

    def value_tile(j):
        return jnp.clip(j - 1, 0, tiles - 1)

    def conv_tile(j):
        return jnp.where(j == 0, tiles, value_tile(j))

    def weight_tile(j):
        return jnp.where(j < tiles, tiles + j, jnp.minimum(j - tiles, tiles - 1))

    def out_tile(j):
        return jnp.maximum(j - tiles - 1, 0)

    def shape(dims, dtype):
        return jax.ShapeDtypeStruct(dims, dtype)

    row2 = lambda a: a.reshape(1, -1)
    once = dict(pipeline_mode=pl.Buffered(1))
    outs = pl.pallas_call(
        functools.partial(front_kernel, *sizes),
        name="front",
        grid=(1 + 2 * tiles,),
        in_specs=[
            whole((length, width), **once),
            pl.BlockSpec((TILE, width), lambda j: (weight_tile(j), 0)),
            pl.BlockSpec((TILE, width), lambda j: (2 * tiles, 0), **once),
            pl.BlockSpec((heads, width), lambda j: ((inner + conv_width) // heads, 0), **once),
            pl.BlockSpec((4, TILE), lambda j: (0, conv_tile(j))),
            pl.BlockSpec((1, TILE), lambda j: (0, conv_tile(j))),
            whole((1, heads)),
            whole((1, heads)),
            whole((1, heads)),
        ],
        out_specs=[
            pl.BlockSpec((length, TILE), lambda j: (0, out_tile(j))),
            pl.BlockSpec((length, TILE), lambda j: (0, conv_tile(j))),
            pl.BlockSpec((length, TILE), lambda j: (0, conv_tile(j))),
            pl.BlockSpec((length, TILE), lambda j: (0, out_tile(j))),
            pl.BlockSpec((length, TILE), lambda j: (0, out_tile(j))),
            pl.BlockSpec((length, TILE), lambda j: (0, out_tile(j))),
            pl.BlockSpec((length, TILE), lambda j: (0, out_tile(j))),
            pl.BlockSpec((chunks, state, TILE), lambda j: (0, 0, value_tile(j))),
            pl.BlockSpec((chunks, state, TILE), lambda j: (0, 0, value_tile(j))),
            whole((count, 2, state, 128)),
            whole((groups, CHUNK, 128)),
            whole((4 * groups, 128)),
            pl.BlockSpec(memory_space=pltpu.SMEM),
        ],
        out_shape=[
            shape((length, inner), BF16),
            shape((length, conv_width), BF16),
            shape((length, conv_width), BF16),
            shape((length, inner), BF16),
            shape((length, inner), BF16),
            shape((length, inner), BF16),
            shape((length, inner), BF16),
            shape((chunks, state, inner), BF16),
            shape((chunks, state, inner), BF16),
            shape((count, 2, state, 128), BF16),
            shape((groups, CHUNK, 128), F32),
            shape((4 * groups, 128), F32),
            shape((groups,), F32),
        ],
        scratch_shapes=[
            pltpu.VMEM((length + 2 * HALO, width), BF16),
            pltpu.VMEM((chunks * (CHUNK + 48), TILE), F32),
            pltpu.VMEM((chunks * (CHUNK + 48), TILE), F32),
            pltpu.VMEM((length, TILE), F32),
            pltpu.VMEM((length, TILE), F32),
            pltpu.VMEM((8, 128), F32),
        ]
        + [pltpu.VMEM((groups, CHUNK, 256), BF16)] * 4
        + [pltpu.VMEM((2, chunks, state, TILE), F32)]
        + [pltpu.VMEM((length, CHUNK + state), BF16)] * 2
        + [pltpu.VMEM((chunks * state, CHUNK), BF16)] * 2
        + [pltpu.VMEM((32, 128), BF16)]
        + [
            pltpu.VMEM((2, tiles, chunks, CHUNK + state, TILE), BF16),
            pltpu.VMEM((2, tiles, length, TILE), BF16),
            pltpu.VMEM((count, 2, state + 16, 128), BF16),
            pltpu.VMEM((16, width), BF16),
            pltpu.VMEM((16, width), BF16),
        ]
        + [pltpu.VMEM((count // 2, 2, state + 16, 128), BF16)] * 3
        + [pltpu.VMEM((count // 2, 2, state, 128), BF16)] * 4
        + [pltpu.SemaphoreType.DMA((n,)) for n in (2, 2, tiles // 2, tiles // 2)]
        + [pltpu.SemaphoreType.DMA((count // 2,))] * 4
        + [pltpu.SemaphoreType.DMA((n,)) for n in (count // 2, count // 2, 2)],
        compiler_params=pltpu.CompilerParams(collective_id=0, has_side_effects=True, vmem_limit_bytes=VMEM),
    )(
        hidden, in_weight.T, in_weight.T, in_weight.T, conv_weight, row2(conv_bias), row2(step_bias), row2(decay_rate),
        row2(skip_gain),
    )
    gate, xf, xb, yf, yb, gf, gb, sf, sb, entering, step, off, span = outs
    anywhere = pl.BlockSpec(memory_space=pl.ANY)
    block = pl.BlockSpec((ROWS, inner), lambda j: (j, 0))
    c_block = pl.BlockSpec((ROWS, state), lambda j: (j, inner // state + 1))
    return pl.pallas_call(
        functools.partial(back_kernel, *sizes),
        name="back",
        grid=(length // ROWS,),
        in_specs=[
            pl.BlockSpec(memory_space=pltpu.SMEM),
            block, block, block, block, c_block, c_block,
            whole((count, 2, state, 128), **once),
            pl.BlockSpec((ROWS, width), lambda j: (j, 0)),
            whole((inner, width), **once),
            whole((1, inner)),
            whole((1, heads)),
            whole((1, heads)),
            whole((4 * groups, 128)),
        ]
        + [anywhere] * 6,
        out_specs=pl.BlockSpec((ROWS, width), lambda j: (j, 0)),
        out_shape=shape((length, width), BF16),
        scratch_shapes=[
            pltpu.VMEM((ROWS, inner), F32),
            pltpu.VMEM((ROWS, inner), F32),
            pltpu.VMEM((ROWS, 128), F32),
            pltpu.VMEM((ROWS, 128), F32),
            pltpu.VMEM((ROWS, inner), BF16),
            pltpu.VMEM((width // 128, ROWS, 128), F32),
            pltpu.VMEM((8, 128), F32),
            pltpu.VMEM((CHUNK, conv_width), BF16),
            pltpu.VMEM((state, inner), BF16),
            pltpu.VMEM((CHUNK, 128), F32),
            pltpu.VMEM((CHUNK, inner), BF16),
            pltpu.SemaphoreType.DMA((4,)),
        ],
        compiler_params=pltpu.CompilerParams(vmem_limit_bytes=VMEM),
    )(
        span, yf, yb, gf, gb, xf, xb, entering, hidden, out_weight, row2(norm_gain), row2(decay_rate),
        row2(skip_gain), off, gate, xf, xb, sf, sb, step,
    )


def solution(mesh):
    return jax.shard_map(
        local,
        mesh=mesh,
        in_specs=(P(("dp", "ctx"), None), P(), P(), P(), P(), P(), P(), P(), P()),
        out_specs=P(("dp", "ctx"), None),
        check_vma=False,
    )
```

```python
import functools

import jax
import jax.numpy as jnp
from jax import lax
from jax.experimental import pallas as pl
from jax.experimental.pallas import tpu as pltpu
from jax.sharding import PartitionSpec as P

CHUNK = 128
TILE = 256
HALO = 8
ROWS = 256
LIMIT = 40.0
VMEM = 66_000_000
MESH = pl.DeviceIdType.MESH
HIGHEST = lax.Precision.HIGHEST
F32 = jnp.float32
BF16 = jnp.bfloat16


def dot(a, b):
    return jnp.dot(a, b, preferred_element_type=F32)


def dot_nt(a, b):
    return lax.dot_general(a, b, (((1,), (1,)), ((), ())), preferred_element_type=F32)


def silu_of_half(half):
    return half + half * jnp.tanh(half)


def silu(x):
    return silu_of_half(0.5 * x)


def iota(shape, dim):
    return lax.broadcasted_iota(jnp.int32, shape, dim)


def iota_mod(shape, dim, mod):
    return lax.rem(iota(shape, dim), mod)


def time_of(index):
    return lax.rem(index, 8) * (CHUNK // 8) + lax.div(index, 8)


def triangle(lower):
    row, column = time_of(iota((CHUNK, CHUNK), 0)), time_of(iota((CHUNK, CHUNK), 1))
    return row >= column if lower else row <= column


def high_low(x):
    high = x.astype(BF16)
    return jnp.concatenate([high, (x - high.astype(F32)).astype(BF16)], 1)


def three_terms(x):
    high = x.astype(BF16).astype(F32)
    middle = (x - high).astype(BF16).astype(F32)
    return [high, middle, x - high - middle]


def spread_matrix(first, head_dim):
    row, column = iota((128, TILE), 0), iota((128, TILE), 1)
    half = jnp.where(row == first + lax.div(column, head_dim), 1.0, 0.0).astype(BF16)
    return jnp.concatenate([half, half], 0)


def front_kernel(
    heads, head_dim, state, inner, x_ref, w_ref, wbc_ref, wdt_ref, cw_ref, cb_ref, bias_ref, decay_ref, skip_ref,
    gate_ref, xf_ref, xb_ref, yf_ref, yb_ref, gf_ref, gb_ref, sf_ref, sb_ref, in_ref, step_ref, off_ref, span_ref,
    hx, xs0, xs1, gate0, gate1, par, wf, wb, of, ob, update, gcf, gcb, btf, btb, small, rhs, kept_x, ends,
    follow, before_me, paired, chip, arrived, answers, entering, other, landed,
    halo_out, halo_in, pair_out, pair_in, first_out, first_in, second_out, second_in, back_out, back_in, own_sem,
):
    length = x_ref.shape[0]
    chunks = length // CHUNK
    tiles = inner // TILE
    packs = 128 // heads
    groups = off_ref.shape[0] // 4
    edge = 24
    span = CHUNK + 2 * edge
    j = pl.program_id(0)
    count = lax.axis_size("ctx")
    me = lax.axis_index("ctx")
    core, mine = lax.rem(me, 2), lax.div(me, 2)
    partner = me + 1 - 2 * core
    low = core == 0
    peers = count // 2
    chips = [lax.rem(mine + d, peers) for d in range(1, peers)]
    half_tiles = tiles // 2
    per_tile = TILE // 128

    def send(src, dst, out_sem, in_sem, peer):
        return pltpu.make_async_remote_copy(
            src_ref=src, dst_ref=dst, send_sem=out_sem, recv_sem=in_sem, device_id={"ctx": peer}, device_id_type=MESH
        )

    def halos():
        edge_rows = follow.shape[0]
        return [
            send(x_ref.at[:edge_rows], follow, halo_out.at[0], halo_in.at[0], lax.rem(me + count - 1, count)),
            send(
                x_ref.at[length - edge_rows :], before_me, halo_out.at[1], halo_in.at[1], lax.rem(me + 1, count)
            ),
        ]

    def pair_copy(t):
        at = pl.ds(t * per_tile, per_tile)
        slot = lax.rem(t, half_tiles)
        return send(
            ends.at[at], paired.at[pl.ds(slot * per_tile, per_tile)], pair_out.at[slot], pair_in.at[slot], partner
        )

    def total(ref, k):
        rows = ref[k, 0, state : state + 16, :].astype(F32)
        return rows[0:1] + rows[1:2] + rows[2:3]

    def first_copy(k):
        return send(chip.at[k], arrived.at[mine], first_out.at[k], first_in.at[mine], 2 * k + core)

    def combine(t):
        slot = lax.rem(t, half_tiles)
        pair_copy(t).wait_recv()
        for half in range(per_tile):
            k = slot * per_tile + half
            at = core * peers + k
            t_own, t_part = total(ends, at), total(paired, k)
            f_own, f_part = jnp.exp(t_own), jnp.exp(t_part)
            one = jnp.ones_like(f_own)
            own0, part0 = ends[at, 0, :state, :].astype(F32), paired[k, 0, :state, :].astype(F32)
            own1, part1 = ends[at, 1, :state, :].astype(F32), paired[k, 1, :state, :].astype(F32)
            chip[k, 0, :state, :] = (
                own0 * jnp.where(low, f_part, one) + part0 * jnp.where(low, one, f_own)
            ).astype(BF16)
            chip[k, 1, :state, :] = (
                own1 * jnp.where(low, one, f_part) + part1 * jnp.where(low, f_own, one)
            ).astype(BF16)
            extra = jnp.concatenate(three_terms(t_own + t_part) + [jnp.zeros((13, 128), F32)], 0).astype(BF16)
            chip[k, 0, state:, :] = extra
            chip[k, 1, state:, :] = extra

            @pl.when(k != mine)
            def _():
                first_copy(k).start()

            @pl.when(k == mine)
            def _():
                pltpu.make_async_copy(chip.at[k], arrived.at[k], own_sem.at[0]).start()

    def second_copy(k):
        return send(answers.at[k], entering.at[mine], second_out.at[k], second_in.at[mine], 2 * k + core)

    def scan():
        pltpu.make_async_copy(chip.at[mine], arrived.at[mine], own_sem.at[0]).wait()
        for k in chips:
            send(chip.at[k], arrived.at[k], first_out.at[k], first_in.at[k], 2 * k + core).wait_recv()
        for strand, order in ((0, list(range(peers))), (1, list(reversed(range(peers))))):
            running = jnp.zeros((state, 128), F32)
            for k in order:
                answers[k, strand] = running.astype(BF16)
                if k != order[-1]:
                    running = jnp.exp(total(arrived, k)) * running + arrived[k, strand, :state, :].astype(F32)
        for k in chips:
            second_copy(k).start()
        pltpu.make_async_copy(answers.at[mine], entering.at[mine], own_sem.at[1]).start()

    def back_copy(k):
        return send(other.at[k], landed.at[k], back_out.at[k], back_in.at[k], partner)

    def enter():
        pltpu.make_async_copy(answers.at[mine], entering.at[mine], own_sem.at[1]).wait()

        def one_pair(d, _):
            k = lax.rem(mine + d, peers)

            @pl.when(d > 0)
            def _():
                send(answers.at[k], entering.at[k], second_out.at[k], second_in.at[k], 2 * k + core).wait_recv()

            at = core * peers + k
            f_own, f_part = jnp.exp(total(ends, at)), jnp.exp(total(paired, k))
            one, none = jnp.ones_like(f_own), jnp.zeros_like(f_own)
            for strand, early in ((0, low), (1, jnp.logical_not(low))):
                chip_in = entering[k, strand].astype(F32)
                scale, add = jnp.where(early, one, f_part), jnp.where(early, none, one)
                in_ref[at, strand] = (scale * chip_in + add * paired[k, strand, :state, :].astype(F32)).astype(BF16)
                scale, add = jnp.where(early, f_own, one), jnp.where(early, one, none)
                other[k, strand] = (scale * chip_in + add * ends[at, strand, :state, :].astype(F32)).astype(BF16)
            back_copy(k).start()
            return 0

        lax.fori_loop(0, peers, one_pair, 0)

    def finish():
        def one_pair(k, _):
            back_copy(k).wait()
            in_ref[(1 - core) * peers + k] = landed[k]
            return 0

        lax.fori_loop(0, peers, one_pair, 0)
        for copy in halos():
            copy.wait_send()
        for slot in range(half_tiles):
            pair_copy((1 - core) * half_tiles + slot).wait_send()
        for k in chips:
            first_copy(k).wait_send()
            second_copy(k).wait_send()

    def keep_rows(xs, out):
        for c in range(chunks):
            xs[c * span + edge : c * span + edge + CHUNK] = out[c * CHUNK : (c + 1) * CHUNK]

    def project(weights, xs):
        out = dot_nt(hx[...], weights[...])
        keep_rows(xs, out)
        join(xs, out[length:])

    def join(xs, out):
        sub = iota((8, TILE), 0)

        def rolled(c, r, by):
            at = c * span + edge + r * 8
            return pltpu.roll(xs[at : at + 8], by, 0)

        for p in range(3):
            r = CHUNK // 8 - 3 + p
            before = jnp.broadcast_to(out[2 * HALO - 3 + p : 2 * HALO - 2 + p], (8, TILE))
            for c in range(chunks):
                mine = rolled(c, r, 1)
                xs[c * span + p * 8 : c * span + p * 8 + 8] = jnp.where(sub == 0, before, mine)
                before = mine
            after = jnp.broadcast_to(out[p : p + 1], (8, TILE))
            for c in reversed(range(chunks)):
                mine = rolled(c, p, 7)
                at = c * span + edge + CHUNK + p * 8
                xs[at : at + 8] = jnp.where(sub == 7, after, mine)
                after = mine

    conv_at = jnp.where(j == 0, tiles, jnp.clip(j - 1, 0, tiles - 1)) * per_tile
    bias = jnp.concatenate([cb_ref[pl.ds(conv_at + n, 1), :] for n in range(per_tile)], 1)

    def convolved(xs, c):
        at = c * span + edge
        taps = [0.5 * cw_ref[k : k + 1, :] for k in range(4)]
        base = xs[at : at + CHUNK] * taps[3] + 0.5 * bias
        forward, backward = base, base
        for k in range(1, 4):
            forward = forward + xs[at - 8 * k : at - 8 * k + CHUNK] * taps[3 - k]
            backward = backward + xs[at + 8 * k : at + 8 * k + CHUNK] * taps[3 - k]
        return silu_of_half(forward), silu_of_half(backward)

    @pl.when(j == 0)
    def _():
        barrier = pltpu.get_barrier_semaphore()
        beside = lax.rem(me + count - 1 + 2 * core, count)
        for peer in [partner, beside] + [2 * k + core for k in chips]:
            pl.semaphore_signal(barrier, inc=1, device_id={"ctx": peer}, device_id_type=MESH)
        pl.semaphore_wait(barrier, peers + 1)
        for copy in halos():
            copy.start()
        order = jnp.where(time_of(iota((CHUNK, CHUNK), 0)) == iota((CHUNK, CHUNK), 1), 1.0, 0.0).astype(BF16)
        for c in range(chunks):
            rows = slice(c * CHUNK, (c + 1) * CHUNK)
            hx[rows] = dot(order, x_ref[rows]).astype(BF16)
        par[...] = jnp.zeros_like(par)
        for q in range(packs):
            par[0:1, q * heads : (q + 1) * heads] = bias_ref[...]
            par[1:2, q * heads : (q + 1) * heads] = decay_ref[...]
        par[2:3, :heads] = skip_ref[...]
        lower = jnp.where(triangle(True), 1.0, 0.0)
        upper = jnp.where(triangle(False), 1.0, 0.0)
        lane1 = iota((1, 128), 1)
        wdt = jnp.concatenate([wdt_ref[...], jnp.zeros((128 - heads, wdt_ref.shape[1]), BF16)], 0)
        all_raw = dot_nt(hx[:length], wdt)
        keep_rows(xs1, dot_nt(hx[:length], wbc_ref[...]))
        totals = []
        for g in range(groups):
            members = range(g * packs, min((g + 1) * packs, chunks))
            raw = jnp.zeros((CHUNK, 128), F32)
            for q, c in enumerate(members):
                one = all_raw[c * CHUNK : (c + 1) * CHUNK]
                raw = raw + (pltpu.roll(one, q * heads, 1) if q else one)
            raw = raw.astype(BF16).astype(F32) + par[0:1, :]
            step = jnp.maximum(raw, 0.0) + jnp.log1p(jnp.exp(-jnp.abs(raw)))
            step = jnp.where(iota((CHUNK, 128), 1) < len(members) * heads, step, 0.0)
            step_ref[g] = step
            rate = -step * par[1:2, :]
            head = jnp.dot(lower, rate, precision=HIGHEST, preferred_element_type=F32)
            tail = jnp.dot(upper, rate, precision=HIGHEST, preferred_element_type=F32)
            total = head[CHUNK - 1 :]
            wf[g] = high_low(step * jnp.exp(jnp.minimum(total - head, 0.0)))
            wb[g] = high_low(step * jnp.exp(jnp.minimum(total - tail, 0.0)))
            of[g] = high_low(jnp.exp(jnp.minimum(head - total, 80.0)))
            ob[g] = high_low(jnp.exp(jnp.minimum(tail - total, 80.0)))
            totals.append(total)
            span_ref[g] = -jnp.min(total)

        def wide8(x):
            return jnp.broadcast_to(x, (8, 128))

        def both(x):
            w = wide8(x)
            for q in range(1, packs):
                w = w + pltpu.roll(wide8(x), q * heads, 1)
            return w[0:1]

        lane8 = iota((8, 128), 1)
        sums = [both(t) for t in totals]
        slab = sums[0]
        for t in sums[1:]:
            slab = slab + t
        reach = []
        for g in range(groups):
            t8 = wide8(totals[g])
            early, late = jnp.zeros((8, 128), F32), jnp.zeros((8, 128), F32)
            for q in range(1, packs):
                early = early + jnp.where(lane8 >= q * heads, pltpu.roll(t8, q * heads, 1), 0.0)
                late = late + jnp.where(lane8 < 128 - q * heads, pltpu.roll(t8, 128 - q * heads, 1), 0.0)
            early, late = early[0:1], late[0:1]
            for k in range(groups):
                if k < g:
                    early = early + sums[k]
                if k > g:
                    late = late + sums[k]
            off_ref[g : g + 1, :] = early
            off_ref[groups + g : groups + g + 1, :] = late
            off_ref[2 * groups + 2 * g : 2 * groups + 2 * g + 2, :] = jnp.zeros((2, 128), F32)
            reach.append((jnp.exp(early + totals[g]), jnp.exp(late + totals[g])))
        lines = []
        for g in range(groups):
            lines += three_terms(jnp.exp(totals[g]))
        lines += three_terms(slab) + three_terms(par[2:3, :])
        for strand in range(2):
            for g in range(groups):
                lines += three_terms(reach[g][strand])
        lines.append(jnp.zeros((small.shape[0] - len(lines), 128), F32))
        small[...] = jnp.concatenate(lines, 0).astype(BF16)
        for copy in halos():
            copy.wait_recv()
        first_row = jnp.where(me == count - 1, 0.0, 1.0)
        last_row = jnp.where(me == 0, 0.0, 1.0)
        hx[length:] = jnp.concatenate(
            [
                follow[...].astype(F32)[:HALO] * first_row,
                before_me[...].astype(F32)[before_me.shape[0] - HALO :] * last_row,
            ],
            0,
        ).astype(BF16)
        join(xs1, dot_nt(hx[length:], wbc_ref[...]))
        for c in range(chunks):
            rows = slice(c * CHUNK, (c + 1) * CHUNK)
            forward, backward = convolved(xs1, c)
            for value, out, gc, bt, keep in (
                (forward, xf_ref, gcf, btf, triangle(True)),
                (backward, xb_ref, gcb, btb, triangle(False)),
            ):
                rounded = value.astype(BF16)
                out[rows, :] = rounded
                b_part, c_part = rounded[:, :state], rounded[:, state:]
                gc[rows, :CHUNK] = jnp.where(keep, dot_nt(c_part, b_part), 0.0).astype(BF16)
                gc[rows, CHUNK:] = c_part
                bt[rows, :] = value[:, :state].T.astype(BF16)
        project(w_ref, xs0)

    first = lax.rem(j - 1, tiles) * (TILE // head_dim)

    @pl.when((j >= 2) & (j <= tiles + 1) & (lax.div(j - 2, half_tiles) == core))
    def _():
        combine(j - 2)

    @pl.when(j == tiles + core * half_tiles)
    def _():
        scan()

    @pl.when((j == tiles + half_tiles) & low)
    def _():
        enter()

    def line_of(lines, q, k):
        rows = lines[q][3 * k : 3 * k + 3]
        return rows[0:1] + rows[1:2] + rows[2:3]

    def gating(gate):
        gate[...] = dot_nt(hx[:length], w_ref[...])

    def values_step(xs):
        t = j - 1
        spreads = [spread_matrix(first + q * heads, head_dim) for q in range(packs)]
        lines = [dot(small[...], spread[:128]) for spread in spreads]
        fade = [line_of(lines, c % packs, c // packs) for c in range(chunks)]
        slab = line_of(lines, 0, groups)

        def summarise(c, pair):
            for strand, (bt, scaled) in enumerate(zip((btf, btb), pair)):
                update[strand, c] = dot(bt[c * CHUNK : (c + 1) * CHUNK, :], scaled)

        scaled = None
        for c in range(chunks):
            rows = slice(c * CHUNK, (c + 1) * CHUNK)
            weights = [dot(w[c // packs], spreads[c % packs]) for w in (wf, wb)]
            if scaled is not None:
                summarise(c - 1, scaled)
            scaled = []
            for strand, (value, x_out) in enumerate(zip(convolved(xs, c), (xf_ref, xb_ref))):
                rounded = value.astype(BF16)
                x_out[rows, :] = rounded
                kept_x[strand, t, rows] = rounded
                scaled.append((value * weights[strand]).astype(BF16))
                rhs[strand, t, c, :CHUNK] = scaled[strand]
        summarise(chunks - 1, scaled)
        extra = jnp.concatenate(three_terms(slab) + [jnp.zeros((13, TILE), F32)], 0).astype(BF16)
        for strand, (order, s_ref) in enumerate(((range(chunks), sf_ref), (reversed(range(chunks)), sb_ref))):
            running = jnp.zeros((state, TILE), F32)
            for c in order:
                decayed = running * fade[c]
                s_ref[c] = running.astype(BF16)
                rhs[strand, t, c, CHUNK:] = decayed.astype(BF16)
                running = decayed + update[strand, c]
            for half in range(per_tile):
                lanes = slice(half * 128, (half + 1) * 128)
                ends[t * per_tile + half, strand, :state, :] = running[:, lanes].astype(BF16)
                ends[t * per_tile + half, strand, state:, :] = extra[:, lanes]

    @pl.when((j > 0) & (j < tiles) & (lax.rem(j, 2) == 1))
    def _():
        project(w_ref, xs1)
        values_step(xs0)

    @pl.when((j > 0) & (j < tiles) & (lax.rem(j, 2) == 0))
    def _():
        project(w_ref, xs0)
        values_step(xs1)

    @pl.when(j == tiles)
    def _():
        gating(gate0)
        values_step(xs1)

    @pl.when((j > 0) & (j <= tiles) & (lax.div(j - 1, half_tiles) != core))
    def _():
        pair_copy(j - 1).start()

    def outputs_step(gate):
        t = j - 1 - tiles
        spreads = [spread_matrix(first + q * heads, head_dim) for q in range(packs)]
        lines = [dot(small[...], spread[:128]) for spread in spreads]
        skip = line_of(lines, 0, groups + 1)
        for c in range(chunks):
            rows = slice(c * CHUNK, (c + 1) * CHUNK)
            raw = gate[rows]
            gate_ref[rows, :] = raw.astype(BF16)
            open_gate = silu(raw)
            for strand, (y_ref, g_ref, gc, o) in enumerate(
                ((yf_ref, gf_ref, gcf, of), (yb_ref, gb_ref, gcb, ob))
            ):
                scale = dot(o[c // packs], spreads[c % packs]) * open_gate
                mixed = dot(gc[rows, :], rhs[strand, t, c])
                y = mixed * scale + (skip * open_gate) * kept_x[strand, t, rows].astype(F32)
                y_ref[rows, :] = y.astype(BF16)
                reach = line_of(lines, c % packs, (strand + 1) * groups + 2 + c // packs)
                g_ref[rows, :] = (scale * reach).astype(BF16)

    @pl.when((j > tiles) & (j < 2 * tiles) & (lax.rem(j, 2) == 1))
    def _():
        gating(gate1)
        outputs_step(gate0)

    @pl.when((j > tiles) & (j < 2 * tiles) & (lax.rem(j, 2) == 0))
    def _():
        gating(gate0)
        outputs_step(gate1)

    @pl.when(j == 2 * tiles)
    def _():
        outputs_step(gate1)

    @pl.when(j == 2 * tiles)
    def _():
        @pl.when(jnp.logical_not(low))
        def _():
            enter()

        finish()


def back_kernel(
    heads, head_dim, state, inner, span_ref, yf_ref, yb_ref, gf_ref, gb_ref, cf_ref, cb_ref, in_ref, x_ref,
    w_ref, gain_ref, decay_ref, skip_ref, off_ref, gate_any, xf_any, xb_any, sf_any, sb_any, step_any,
    out_ref, gf, gb, accf, accb, normed, unshuffled, par, xbuf, sbuf, dtbuf, gatebuf, sem,
):
    rows = out_ref.shape[0]
    i = pl.program_id(0)
    per_block = rows // CHUNK
    packs = 128 // heads
    groups = off_ref.shape[0] // 4
    group = lax.div(i * per_block, packs)
    slot = lax.rem(i * per_block, packs)
    worst = span_ref[group]

    @pl.when(worst <= LIMIT)
    def _():
        total_f = jnp.zeros((rows, 128), F32)
        total_b = jnp.zeros((rows, 128), F32)
        for j in range(inner // TILE):
            lanes = slice(j * TILE, (j + 1) * TILE)

            def strand(y_ref, c_ref, g_ref, s, g):
                entering = jnp.concatenate([in_ref[2 * j, s], in_ref[2 * j + 1, s]], 1)
                y = y_ref[:, lanes].astype(F32) + g_ref[:, lanes].astype(F32) * dot(c_ref[...], entering)
                g[:, lanes] = y
                square = y * y
                return square[:, :128] + square[:, 128:]

            total_f = total_f + strand(yf_ref, cf_ref, gf_ref, 0, gf)
            total_b = total_b + strand(yb_ref, cb_ref, gb_ref, 1, gb)
        accf[...] = total_f
        accb[...] = total_b

    @pl.when(jnp.logical_not(worst <= LIMIT))
    def _():
        par[...] = jnp.zeros_like(par)
        for q in range(packs):
            par[0:1, q * heads : (q + 1) * heads] = decay_ref[...]
            par[1:2, q * heads : (q + 1) * heads] = skip_ref[...]
        accf[...] = jnp.zeros_like(accf)
        accb[...] = jnp.zeros_like(accb)
        for s, (x_any, s_any, g, acc) in enumerate(((xf_any, sf_any, gf, accf), (xb_any, sb_any, gb, accb))):
            keep = triangle(s == 0)
            ones = jnp.where(keep, 1.0, 0.0)

            def one_chunk(k, _):
                c = i * per_block + k
                copies = [
                    pltpu.make_async_copy(x_any.at[pl.ds(c * CHUNK, CHUNK)], xbuf, sem.at[0]),
                    pltpu.make_async_copy(s_any.at[c], sbuf, sem.at[1]),
                    pltpu.make_async_copy(step_any.at[group], dtbuf, sem.at[2]),
                    pltpu.make_async_copy(gate_any.at[pl.ds(c * CHUNK, CHUNK)], gatebuf, sem.at[3]),
                ]
                for copy in copies:
                    copy.start()
                for copy in copies:
                    copy.wait()
                at = pl.ds(pl.multiple_of(k * CHUNK, CHUNK), CHUNK)
                dt = dtbuf[...]
                log_decay = jnp.dot(ones, -dt * par[0:1, :], precision=HIGHEST, preferred_element_type=F32)
                picked = iota(off_ref.shape, 0) == s * groups + group
                offset = jnp.sum(jnp.where(picked, off_ref[...], 0.0), 0, keepdims=True)
                log_t, dt_t = log_decay.T, dt.T
                b_part, c_part = xbuf[:, inner : inner + state], xbuf[:, inner + state :]
                scores = dot_nt(c_part, b_part)
                lane, sub = iota((CHUNK, 128), 1), iota((128, CHUNK), 0)
                lane1 = iota((1, 128), 1)
                left = lane < head_dim

                def pair(q, _):
                    cols = pl.ds(pl.multiple_of(q * 128, 128), 128)
                    v = xbuf[:, cols]
                    outs, ups, skips, offsets = [], [], [], []
                    for half in range(2):
                        h = 2 * q + half + (slot + k) * heads
                        column = jnp.sum(jnp.where(lane == h, log_decay, 0.0), 1, keepdims=True)
                        line = jnp.sum(jnp.where(sub == h, log_t, 0.0), 0, keepdims=True)
                        dt_line = jnp.sum(jnp.where(sub == h, dt_t, 0.0), 0, keepdims=True)
                        decay = jnp.where(keep, jnp.exp(jnp.minimum(column - line, 0.0)), 0.0)
                        outs.append(dot((decay * scores * dt_line).astype(BF16), v))
                        ups.append(jnp.exp(column))
                        skips.append(jnp.sum(jnp.where(lane1 == h, par[1:2, :], 0.0), 1, keepdims=True))
                        offsets.append(jnp.sum(jnp.where(lane1 == h, offset, 0.0), 1, keepdims=True))
                    shift = jnp.where(lane1 < head_dim, offsets[0], offsets[1])
                    entering = sbuf[:, cols].astype(F32) + jnp.exp(shift) * in_ref[q, s].astype(F32)
                    carried = dot(c_part, entering.astype(BF16))
                    y = jnp.where(left, outs[0], outs[1]) + jnp.where(left, ups[0], ups[1]) * carried
                    y = y + jnp.where(lane1 < head_dim, skips[0], skips[1]) * v.astype(F32)
                    y = y * silu(gatebuf[:, cols].astype(F32))
                    g[at, cols] = y
                    acc[at, :] += y * y
                    return 0

                lax.fori_loop(0, heads // 2, pair, 0)
                return 0

            lax.fori_loop(0, per_block, one_chunk, 0)

    scale_f = lax.rsqrt(jnp.sum(accf[...], 1, keepdims=True) * (1.0 / inner) + 1e-05)
    scale_b = lax.rsqrt(jnp.sum(accb[...], 1, keepdims=True) * (1.0 / inner) + 1e-05)
    for j in range(inner // TILE):
        lanes = slice(j * TILE, (j + 1) * TILE)
        gain = jnp.concatenate([gain_ref[n : n + 1, :] for n in range(2 * j, 2 * j + 2)], 1)
        value = (gf[:, lanes] * scale_f + gb[:, lanes] * scale_b) * gain
        normed[:, lanes] = value.astype(BF16)
    steps = CHUNK // 8
    product = dot(normed[...], w_ref[...])
    for n in range(w_ref.shape[1] // 128):
        lanes = slice(n * 128, (n + 1) * 128)
        for k in range(per_block):
            for r in range(steps):
                at = k * CHUNK + r * 8
                unshuffled[n, pl.ds(k * CHUNK + r, 8, stride=steps), :] = product[at : at + 8, lanes]
        out_ref[:, lanes] = (x_ref[:, lanes].astype(F32) + unshuffled[n]).astype(BF16)


def local(hidden, in_weight, conv_weight, conv_bias, step_bias, decay_rate, skip_gain, norm_gain, out_weight):
    length, width = hidden.shape
    heads = step_bias.shape[0]
    inner = out_weight.shape[0]
    head_dim = inner // heads
    conv_width = conv_weight.shape[1]
    state = (conv_width - inner) // 2
    chunks = length // CHUNK
    tiles = inner // TILE
    count = lax.axis_size("ctx")
    groups = -(-chunks * heads // 128)
    sizes = (heads, head_dim, state, inner)

    def whole(shape, **kw):
        return pl.BlockSpec(shape, lambda j: (0,) * len(shape), **kw)

    def value_tile(j):
        return jnp.clip(j - 1, 0, tiles - 1)

    def conv_tile(j):
        return jnp.where(j == 0, tiles, value_tile(j))

    def weight_tile(j):
        return jnp.where(j < tiles, tiles + j, jnp.minimum(j - tiles, tiles - 1))

    def out_tile(j):
        return jnp.maximum(j - tiles - 1, 0)

    def shape(dims, dtype):
        return jax.ShapeDtypeStruct(dims, dtype)

    row2 = lambda a: a.reshape(1, -1)
    once = dict(pipeline_mode=pl.Buffered(1))
    outs = pl.pallas_call(
        functools.partial(front_kernel, *sizes),
        name="front",
        grid=(1 + 2 * tiles,),
        in_specs=[
            whole((length, width), **once),
            pl.BlockSpec((TILE, width), lambda j: (weight_tile(j), 0)),
            pl.BlockSpec((TILE, width), lambda j: (2 * tiles, 0), **once),
            pl.BlockSpec((heads, width), lambda j: ((inner + conv_width) // heads, 0), **once),
            pl.BlockSpec((4, TILE), lambda j: (0, conv_tile(j))),
            whole((conv_width // 128, 128)),
            whole((1, heads)),
            whole((1, heads)),
            whole((1, heads)),
        ],
        out_specs=[
            pl.BlockSpec((length, TILE), lambda j: (0, out_tile(j))),
            pl.BlockSpec((length, TILE), lambda j: (0, conv_tile(j))),
            pl.BlockSpec((length, TILE), lambda j: (0, conv_tile(j))),
            pl.BlockSpec((length, TILE), lambda j: (0, out_tile(j))),
            pl.BlockSpec((length, TILE), lambda j: (0, out_tile(j))),
            pl.BlockSpec((length, TILE), lambda j: (0, out_tile(j))),
            pl.BlockSpec((length, TILE), lambda j: (0, out_tile(j))),
            pl.BlockSpec((chunks, state, TILE), lambda j: (0, 0, value_tile(j))),
            pl.BlockSpec((chunks, state, TILE), lambda j: (0, 0, value_tile(j))),
            whole((count, 2, state, 128)),
            whole((groups, CHUNK, 128)),
            whole((4 * groups, 128)),
            pl.BlockSpec(memory_space=pltpu.SMEM),
        ],
        out_shape=[
            shape((length, inner), BF16),
            shape((length, conv_width), BF16),
            shape((length, conv_width), BF16),
            shape((length, inner), BF16),
            shape((length, inner), BF16),
            shape((length, inner), BF16),
            shape((length, inner), BF16),
            shape((chunks, state, inner), BF16),
            shape((chunks, state, inner), BF16),
            shape((count, 2, state, 128), BF16),
            shape((groups, CHUNK, 128), F32),
            shape((4 * groups, 128), F32),
            shape((groups,), F32),
        ],
        scratch_shapes=[
            pltpu.VMEM((length + 2 * HALO, width), BF16),
            pltpu.VMEM((chunks * (CHUNK + 48), TILE), F32),
            pltpu.VMEM((chunks * (CHUNK + 48), TILE), F32),
            pltpu.VMEM((length, TILE), F32),
            pltpu.VMEM((length, TILE), F32),
            pltpu.VMEM((8, 128), F32),
        ]
        + [pltpu.VMEM((groups, CHUNK, 256), BF16)] * 4
        + [pltpu.VMEM((2, chunks, state, TILE), F32)]
        + [pltpu.VMEM((length, CHUNK + state), BF16)] * 2
        + [pltpu.VMEM((chunks * state, CHUNK), BF16)] * 2
        + [pltpu.VMEM((32, 128), BF16)]
        + [
            pltpu.VMEM((2, tiles, chunks, CHUNK + state, TILE), BF16),
            pltpu.VMEM((2, tiles, length, TILE), BF16),
            pltpu.VMEM((count, 2, state + 16, 128), BF16),
            pltpu.VMEM((16, width), BF16),
            pltpu.VMEM((16, width), BF16),
        ]
        + [pltpu.VMEM((count // 2, 2, state + 16, 128), BF16)] * 3
        + [pltpu.VMEM((count // 2, 2, state, 128), BF16)] * 4
        + [pltpu.SemaphoreType.DMA((n,)) for n in (2, 2, tiles // 2, tiles // 2)]
        + [pltpu.SemaphoreType.DMA((count // 2,))] * 4
        + [pltpu.SemaphoreType.DMA((n,)) for n in (count // 2, count // 2, 2)],
        compiler_params=pltpu.CompilerParams(collective_id=0, has_side_effects=True, vmem_limit_bytes=VMEM),
    )(
        hidden, in_weight.T, in_weight.T, in_weight.T, conv_weight, conv_bias.reshape(-1, 128), row2(step_bias), row2(decay_rate),
        row2(skip_gain),
    )
    gate, xf, xb, yf, yb, gf, gb, sf, sb, entering, step, off, span = outs
    anywhere = pl.BlockSpec(memory_space=pl.ANY)
    block = pl.BlockSpec((ROWS, inner), lambda j: (j, 0))
    c_block = pl.BlockSpec((ROWS, state), lambda j: (j, inner // state + 1))
    return pl.pallas_call(
        functools.partial(back_kernel, *sizes),
        name="back",
        grid=(length // ROWS,),
        in_specs=[
            pl.BlockSpec(memory_space=pltpu.SMEM),
            block, block, block, block, c_block, c_block,
            whole((count, 2, state, 128), **once),
            pl.BlockSpec((ROWS, width), lambda j: (j, 0)),
            whole((inner, width), **once),
            whole((inner // 128, 128)),
            whole((1, heads)),
            whole((1, heads)),
            whole((4 * groups, 128)),
        ]
        + [anywhere] * 6,
        out_specs=pl.BlockSpec((ROWS, width), lambda j: (j, 0)),
        out_shape=shape((length, width), BF16),
        scratch_shapes=[
            pltpu.VMEM((ROWS, inner), F32),
            pltpu.VMEM((ROWS, inner), F32),
            pltpu.VMEM((ROWS, 128), F32),
            pltpu.VMEM((ROWS, 128), F32),
            pltpu.VMEM((ROWS, inner), BF16),
            pltpu.VMEM((width // 128, ROWS, 128), F32),
            pltpu.VMEM((8, 128), F32),
            pltpu.VMEM((CHUNK, conv_width), BF16),
            pltpu.VMEM((state, inner), BF16),
            pltpu.VMEM((CHUNK, 128), F32),
            pltpu.VMEM((CHUNK, inner), BF16),
            pltpu.SemaphoreType.DMA((4,)),
        ],
        compiler_params=pltpu.CompilerParams(vmem_limit_bytes=VMEM),
    )(
        span, yf, yb, gf, gb, xf, xb, entering, hidden, out_weight, norm_gain.reshape(-1, 128), row2(decay_rate),
        row2(skip_gain), off, gate, xf, xb, sf, sb, step,
    )


def solution(mesh):
    return jax.shard_map(
        local,
        mesh=mesh,
        in_specs=(P(("dp", "ctx"), None), P(), P(), P(), P(), P(), P(), P(), P()),
        out_specs=P(("dp", "ctx"), None),
        check_vma=False,
    )
```
